32 devices in a mesh: groups: 2 (over y), section: 2 (over core), sp: 4 (over z), blk: 2 (over x).
Axes of the slice: x: 2, y: 2, z: 4, core: 2. Of those that a mesh axis runs over, the one named last changes fastest.
Arguments:
- latent: float32 [2, 12, 64, 128], P('section', ('groups', 'blk'), 'sp'), parts along dimension 1, may hold values from -6 to 6
- queries: bfloat16 [2, 12, 2, 128, 4096], P('section', ('groups', 'blk'), None, 'sp'), parts along dimension 1
- keys: bfloat16 [2, 12, 2, 128, 4096], P('section', ('groups', 'blk'), None, 'sp'), parts along dimension 1
- values: bfloat16 [2, 12, 2, 128, 4096], P('section', ('groups', 'blk'), None, 'sp'), parts along dimension 1, may hold values from -6 to 6
- head_weight: bfloat16 [2, 64, 4096], P('section'), may hold values from -5 to 5
- step_index: int32 [2, 12], P('section', ('groups', 'blk')), parts along dimension 1, may hold values from 0 to 39, as said below
- skip_flags: int32 [12], P(('groups', 'blk')), parts along dimension 0, may hold values 0 or 1
Outputs:
- velocity: float32 [2, 12, 64, 128], P('section', ('groups', 'blk'), 'sp'), parts along dimension 1
- next_latent: float32 [2, 12, 64, 128], P('section', ('groups', 'blk'), 'sp'), parts along dimension 1
The draws below stay inside these ranges and needn't reach their ends.
There are 2 independent parts, one for each index of `groups`. The reference program is written for one: setup_inputs(seed, part) draws one part's arguments, and reference() takes and returns one part's arrays. A program takes and returns all parts, laid end to end along the dimension named above; an argument that names none is the same for every part. Nothing has to cross between parts.
Inputs may be any that keep to these rules, and one draw needn't show every extreme that they name: `step_index`: row 0 (high-noise section) lies below 25, some videos at 24; row 1 (low-noise section) lies in 25 to 39.
All inputs are finite; a program needn't handle non-finite values. No bound on the sum of `skip_flags` on one device may be relied on, other than what follows from the above.
Results may differ from the reference program's by a relative error of at most 0.0041.
Values may be sent and summed in bfloat16 or wider, within the bound.
No kernel may reach another device: no remote copies, remote signals or barrier semaphores. Data moves between devices by JAX's collectives and lax.ppermute only.
A program may use at most 64 MiB of HBM per device.

```python
import jax
import jax.numpy as jnp
from jax import lax

HD = 128
CH = 64
STEPS = 40
SWITCH = 25
SEQ = 128
VIDEOS = 6
FEAT = 4096


def query_key_pair(key):
    array_shape = (2, VIDEOS, 2, SEQ, FEAT)
    query_key = jax.random.fold_in(key, 11)
    base_key = jax.random.fold_in(key, 12)
    query_draw = jax.random.normal(query_key, array_shape, jnp.float32)
    key_draw = jax.random.normal(base_key, array_shape, jnp.float32)
    return (query_draw, key_draw)


def draw_queries(key, part):
    return query_key_pair(key)[0].astype(jnp.bfloat16)


def draw_keys(key, part):
    return query_key_pair(key)[1].astype(jnp.bfloat16)


def draw_step_index(key, part):
    shuffled = jax.random.permutation(jax.random.fold_in(key, 21), VIDEOS)
    finished = shuffled < (VIDEOS + 1) // 2
    earlier_steps = jax.random.randint(jax.random.fold_in(key, 22), (VIDEOS,), 0, SWITCH - 1)
    earlier_steps = jnp.where(shuffled == VIDEOS - 1, 0, earlier_steps)
    high_steps = jnp.where(finished, SWITCH - 1, earlier_steps)
    low_steps = jax.random.randint(jax.random.fold_in(key, 23), (VIDEOS,), SWITCH, STEPS)
    low_steps = jnp.where(shuffled == VIDEOS - 1, STEPS - 1, low_steps)
    return jnp.stack([high_steps, low_steps]).astype(jnp.int32)


def touch_ends(result, own_key, low, high):
    longest = result.shape.index(max(result.shape))
    spots = []
    for shift in (0, 1):
        where = [jax.random.randint(jax.random.fold_in(own_key, axis), (), 0, length) for axis, length in enumerate(result.shape)]
        where[longest] = (where[longest] + shift) % result.shape[longest]
        spots.append(tuple(where))
    return result.at[spots[0]].set(low).at[spots[1]].set(high)


def levels(key, extent, cuts, least, largest):
    def one(position, parts):
        draws = jax.random.uniform(jax.random.fold_in(jax.random.fold_in(key, 6), position), (parts,), jnp.float32, least / len(cuts), largest / len(cuts))
        return jnp.repeat(jnp.exp(draws), extent[position] // parts).reshape((-1,) + (1,) * (len(extent) - position - 1))

    level = one(*cuts[0])
    for cut in cuts[1:]:
        level = level * one(*cut)
    return level


def centred(rng, extent, deviation, bound, cuts=(), dtype=jnp.bfloat16):
    result = deviation * jax.random.normal(rng, extent, jnp.float32)
    if cuts:
        result = result * levels(rng, extent, cuts, -0.22, 0.18)
    return jnp.clip(result, -bound, bound).astype(dtype)


def setup_inputs(seed: int = 0, part: int = 0) -> dict:
    key_list = jax.random.split(jax.random.key(seed), 8)
    part_splits = jax.random.split(jax.random.fold_in(key_list[7], part), 8)
    return {
        "latent": centred(part_splits[0], (2, VIDEOS, SEQ // 2, 2 * CH), 1.0, 6.0, ((0, 2), (1, 2), (2, 4)), jnp.float32),
        "queries": draw_queries(jax.random.fold_in(jax.random.fold_in(key_list[7], part), 71), part),
        "keys": draw_keys(jax.random.fold_in(jax.random.fold_in(key_list[7], part), 71), part),
        "values": centred(part_splits[3], (2, VIDEOS, 2, SEQ, FEAT), 1.0, 6.0, ((0, 2), (1, 2), (3, 4))),
        "head_weight": centred(key_list[4], (2, CH, FEAT), 0.35, 5.0, ((0, 2),)),
        "step_index": draw_step_index(jax.random.fold_in(jax.random.fold_in(key_list[7], part), 71), part),
        "skip_flags": touch_ends((jax.random.randint(part_splits[6], (VIDEOS,), 0, 2) < 1).astype(jnp.int32), jax.random.fold_in(part_splits[6], 1), 0, 1),
    }


noise_shift = 12.0
high_guidance = 4.0
low_guidance = 3.0


def noise_level(step_now):
    fraction = 1.0 - step_now.astype(jnp.float32) / STEPS
    return noise_shift * fraction / (1.0 + (noise_shift - 1.0) * fraction)


def head_attend(query_rows, key_rows, value_rows):
    scores = lax.dot_general(query_rows, key_rows, (((1,), (1,)), ((), ())), preferred_element_type=jnp.float32) * (HD ** -0.5)
    row_max = jnp.max(scores, axis=1, keepdims=True)
    exponent = jnp.exp(scores - row_max)
    row_total = jnp.sum(exponent, axis=1, keepdims=True)
    weights = (exponent / row_total).astype(jnp.bfloat16)
    return jnp.dot(weights, value_rows, preferred_element_type=jnp.float32).astype(jnp.bfloat16)


def attend_heads(query_part, key_part, value_part):
    item_count, length, feature_width = query_part.shape
    head_count = feature_width // HD

    def by_head(array):
        return array.reshape(item_count, length, head_count, HD).transpose(0, 2, 1, 3).reshape(item_count * head_count, length, HD)

    results = lax.map(lambda triple: head_attend(triple[0], triple[1], triple[2]), (by_head(query_part), by_head(key_part), by_head(value_part)))
    return results.reshape(item_count, head_count, length, HD).transpose(0, 2, 1, 3).reshape(item_count, length, feature_width)


def reference(latent, queries, keys, values, head_weight, step_index, skip_flags):
    flat_queries = queries.reshape(2 * VIDEOS * 2, SEQ, FEAT)
    flat_keys = keys.reshape(2 * VIDEOS * 2, SEQ, FEAT)
    flat_values = values.reshape(2 * VIDEOS * 2, SEQ, FEAT)
    attended = lax.map(lambda triple: attend_heads(triple[0][None], triple[1][None], triple[2][None])[0], (flat_queries, flat_keys, flat_values))
    attended = attended.reshape(2, VIDEOS * 2 * SEQ, FEAT)
    projected = []
    for section_index in range(2):
        projected.append(lax.dot_general(attended[section_index], head_weight[section_index], (((1,), (1,)), ((), ())), preferred_element_type=jnp.float32))
    pass_velocity = jnp.stack(projected).reshape(2, VIDEOS, 2, SEQ // 2, 2 * CH)
    conditional = pass_velocity[:, :, 0]
    unconditional = pass_velocity[:, :, 1]
    scales = jnp.array([high_guidance, low_guidance], jnp.float32).reshape(2, 1, 1, 1)
    guided = unconditional + scales * (conditional - unconditional)
    skipping = jnp.stack([jnp.zeros((VIDEOS,), bool), skip_flags == 1])
    guided = jnp.where(skipping[:, :, None, None], conditional, guided)
    step_size = noise_level(step_index + 1) - noise_level(step_index)
    updated = latent + step_size[:, :, None, None] * guided
    finished = step_index[0] + 1 == SWITCH
    low_next = jnp.where(finished[:, None, None], updated[0], updated[1])
    next_latent = jnp.stack([updated[0], low_next])
    return guided, next_latent
```

```python
import functools

import jax
import jax.numpy as jnp
from jax import lax
from jax.experimental import pallas as pl
from jax.experimental.pallas import tpu as pltpu
from jax.sharding import PartitionSpec as P

HD = 128
CH = 64
STEPS = 40
SWITCH = 25


noise_shift = 12.0
high_guidance = 4.0
low_guidance = 3.0

VMEM = pl.BlockSpec(memory_space=pltpu.VMEM)
SMEM = pl.BlockSpec(memory_space=pltpu.SMEM)


def noise_level(step_now):
    fraction = 1.0 - step_now.astype(jnp.float32) / STEPS
    return noise_shift * fraction / (1.0 + (noise_shift - 1.0) * fraction)


def lanes(index, width):
    return pl.ds(pl.multiple_of(index * width, width), width)


def pack_kernel(count, width, me_ref, q_ref, k_ref, *out_refs):
    me = me_ref[0]
    for s in range(1, count):
        there = lanes(me ^ s, width)
        out_refs[s - 1][:, :, 0:width] = q_ref[:, :, there]
        out_refs[s - 1][:, :, width : 2 * width] = k_ref[:, :, there]


def project_kernel(count, width, me_ref, v_ref, w_ref, *out_refs):
    me = me_ref[0]
    items, rows, _ = v_ref.shape
    pair = 2 * HD
    for s in range(count):
        for p in range(width // pair):
            start = pl.multiple_of((me ^ s) * width + p * pair, pair)
            there = pl.ds(start, pair)
            weight = w_ref[:, there]
            column = lax.broadcasted_iota(jnp.int32, weight.shape, 1)
            zero = jnp.zeros_like(weight)
            stacked = jnp.concatenate(
                [jnp.where(column < HD, weight, zero), jnp.where(column < HD, zero, weight)],
                axis=0,
            )
            value = v_ref[:, :, there].reshape(items * rows, pair)
            product = lax.dot_general(
                value, stacked, (((1,), (1,)), ((), ())), preferred_element_type=jnp.float32
            )
            out_refs[s][:, :, p * 2 * CH : (p + 1) * 2 * CH] = product.astype(
                jnp.bfloat16
            ).reshape(items, rows, 2 * CH)


def score_kernel(count, width, me_ref, q_ref, k_ref, *refs):
    others, out_ref = refs[:-1], refs[-1]
    me = me_ref[0]
    items = q_ref.shape[0]

    def one(i, carry):
        for h in range(width // HD):
            own = pl.ds(pl.multiple_of(me * width + h * HD, HD), HD)
            query = jnp.concatenate(
                [q_ref[i, :, own]] + [r[i, :, h * HD : (h + 1) * HD] for r in others], axis=0
            )
            key = jnp.concatenate(
                [k_ref[i, :, own]]
                + [r[i, :, width + h * HD : width + (h + 1) * HD] for r in others],
                axis=0,
            )
            scores = lax.dot_general(
                query, key, (((1,), (1,)), ((), ())), preferred_element_type=jnp.float32
            ) * (HD ** (-0.5))
            length = scores.shape[1]
            row_max = jnp.max(scores, axis=1, keepdims=True)
            out_ref[i, :, h * length : (h + 1) * length] = jnp.exp(scores - row_max).astype(
                jnp.bfloat16
            )
        return carry

    lax.fori_loop(0, items, one, 0)


def attend_kernel(count, width, scale_ref, skip_ref, e_ref, *refs):
    vw_refs, out_ref, scratch = refs[:count], refs[count], refs[count + 1]
    videos = out_ref.shape[1]
    rows = vw_refs[0].shape[1]
    length = rows * count
    ones = jnp.ones((length, 2 * CH), jnp.bfloat16)

    def one(v, carry):
        sums = []
        for way in range(2):
            i = 2 * v + way
            halves = [None, None]
            for h in range(width // HD):
                p = h // 2
                value = jnp.concatenate(
                    [r[i, :, p * 2 * CH : (p + 1) * 2 * CH] for r in vw_refs], axis=0
                )
                mixed = jnp.dot(
                    e_ref[i, :, h * length : (h + 1) * length],
                    jnp.concatenate([value, ones], axis=1),
                    preferred_element_type=jnp.float32,
                )
                term = mixed[:, : 2 * CH] / mixed[:, 2 * CH :]
                halves[h % 2] = term if halves[h % 2] is None else halves[h % 2] + term
            sums.append(halves[0] + pltpu.roll(halves[1], CH, 1))
        conditional, unconditional = sums
        guided = unconditional + scale_ref[0] * (conditional - unconditional)
        guided = jnp.where(skip_ref[v] == 1, conditional, guided)
        scratch[...] = guided
        even = scratch[pl.ds(0, length // 2, stride=2), :]
        odd = scratch[pl.ds(1, length // 2, stride=2), :]
        column = lax.broadcasted_iota(jnp.int32, even.shape, 1)
        both = jnp.where(column < CH, even, pltpu.roll(odd, CH, 1))
        for s in range(count):
            out_ref[s, v] = both[s * rows // 2 : (s + 1) * rows // 2]
        return carry

    lax.fori_loop(0, videos, one, 0)


def call(kernel, outs, specs, name, scratch=(), flops=0, moved=0):
    return pl.pallas_call(
        kernel,
        out_shape=outs,
        in_specs=specs,
        out_specs=jax.tree.map(lambda _: VMEM, outs),
        scratch_shapes=scratch,
        name=name,
        compiler_params=pltpu.CompilerParams(vmem_limit_bytes=12 << 20),
        cost_estimate=pl.CostEstimate(flops=flops, bytes_accessed=moved, transcendentals=0),
    )


def on_device(count, latent, queries, keys, values, head_weight, step_index, skip_flags):
    section_index = lax.axis_index("section")
    me = lax.axis_index("sp")[None]
    _, videos, _, rows, feature_all = queries.shape
    items = videos * 2
    width = feature_all // count
    heads = width // HD
    length = rows * count
    query = queries[0].reshape(items, rows, feature_all)
    key = keys[0].reshape(items, rows, feature_all)
    value = values[0].reshape(items, rows, feature_all)

    def exchange(array, s):
        return lax.ppermute(array, "sp", [(i, i ^ s) for i in range(count)])

    pack = call(
        functools.partial(pack_kernel, count, width),
        [jax.ShapeDtypeStruct((items, rows, 2 * width), jnp.bfloat16)] * (count - 1),
        [SMEM, VMEM, VMEM],
        "pack",
        moved=8 * items * rows * feature_all,
    )
    packed = pack(me, query, key)
    arrived = [exchange(packed[s - 1], s) for s in range(1, count)]

    project = call(
        functools.partial(project_kernel, count, width),
        [jax.ShapeDtypeStruct((items, rows, heads * CH), jnp.bfloat16)] * count,
        [SMEM, VMEM, VMEM],
        "project",
        flops=8 * items * rows * feature_all * CH,
        moved=3 * items * rows * feature_all,
    )
    projected = project(me, value, head_weight[0])
    projected = [projected[0]] + [exchange(projected[s], s) for s in range(1, count)]

    score = call(
        functools.partial(score_kernel, count, width),
        jax.ShapeDtypeStruct((items, length, heads * length), jnp.bfloat16),
        [SMEM] + [VMEM] * (count + 1),
        "score",
        flops=2 * items * heads * length * length * HD * 4,
        moved=8 * items * rows * feature_all,
    )
    weights = score(me, query, key, *arrived)

    guidance = jnp.where(section_index == 0, jnp.float32(high_guidance), jnp.float32(low_guidance))
    skipping = jnp.where(section_index == 1, skip_flags, 0)
    attend = call(
        functools.partial(attend_kernel, count, width),
        jax.ShapeDtypeStruct((count, videos, rows // 2, 2 * CH), jnp.float32),
        [SMEM, SMEM] + [VMEM] * (count + 1),
        "attend",
        scratch=[pltpu.VMEM((length, 2 * CH), jnp.float32)],
        flops=2 * items * heads * length * length * HD * 4,
        moved=4 * items * rows * feature_all,
    )
    shares = attend(guidance[None], skipping, weights, *projected)
    guided = shares[0]
    for s in range(1, count):
        guided = guided + exchange(shares[s], s)

    step_now = step_index[0]
    step_size = noise_level(step_now + 1) - noise_level(step_now)
    updated = latent[0] + step_size[:, None, None] * guided
    finish_mark = jnp.where(
        (section_index == 0) & (step_now + 1 == SWITCH), jnp.float32(1.0), jnp.float32(0.0)
    )
    arrived_mark = lax.ppermute(finish_mark, "section", [(0, 1)])
    arrived = lax.ppermute(updated, "section", [(0, 1)])
    taking = (section_index == 1) & (arrived_mark > 0.5)
    next_latent = jnp.where(taking[:, None, None], arrived, updated)
    return (guided[None], next_latent[None])


def solution(mesh):
    placed = (
        P("section", ("groups", "blk"), "sp", None),
        P("section", ("groups", "blk"), None, "sp", None),
        P("section", ("groups", "blk"), None, "sp", None),
        P("section", ("groups", "blk"), None, "sp", None),
        P("section", None, None),
        P("section", ("groups", "blk")),
        P(("groups", "blk")),
    )
    return jax.shard_map(
        functools.partial(on_device, mesh.shape["sp"]),
        mesh=mesh,
        in_specs=placed,
        out_specs=(
            P("section", ("groups", "blk"), "sp", None),
            P("section", ("groups", "blk"), "sp", None),
        ),
        check_vma=False,
    )
```

```python
import functools

import jax
import jax.numpy as jnp
from jax import lax
from jax.experimental import pallas as pl
from jax.experimental.pallas import tpu as pltpu
from jax.sharding import PartitionSpec as P

HD = 128
CH = 64
STEPS = 40
SWITCH = 25


noise_shift = 12.0
high_guidance = 4.0
low_guidance = 3.0

VMEM = pl.BlockSpec(memory_space=pltpu.VMEM)
SMEM = pl.BlockSpec(memory_space=pltpu.SMEM)
PAIR = 2 * HD


def noise_level(step_now):
    fraction = 1.0 - step_now.astype(jnp.float32) / STEPS
    return noise_shift * fraction / (1.0 + (noise_shift - 1.0) * fraction)


def dot_last(left, right):
    return lax.dot_general(
        left, right, (((1,), (1,)), ((), ())), preferred_element_type=jnp.float32
    )


def side_by_side(first, second):
    zero = jnp.zeros_like(first)
    return [
        jnp.concatenate([first, zero], axis=1),
        jnp.concatenate([zero, second], axis=1),
    ]


def pack_kernel(count, group, width, me_ref, q_ref, k_ref, *out_refs):
    me = me_ref[0]
    for s in range(1, count):
        start = pl.multiple_of(((me ^ s) & (group - 1)) * width, width)
        there = pl.ds(start, width)
        out_refs[s - 1][:, :, 0:width] = q_ref[:, :, there]
        if s < group:
            out_refs[s - 1][:, :, width : 2 * width] = k_ref[:, :, there]


def project_kernel(group, width, me_ref, v_ref, w_ref, *out_refs):
    me = me_ref[0]
    videos = out_refs[0].shape[0]
    for s in range(group):
        first = ((me ^ s) & (group - 1)) * width
        for p in range(width // PAIR):
            start = pl.multiple_of(first + p * PAIR, PAIR)
            weight = w_ref[:, pl.ds(start, PAIR)]
            for v in range(videos):
                rows = []
                for way in range(2):
                    value = v_ref[2 * v + way, :, pl.ds(start, PAIR)]
                    rows += side_by_side(value[:, :HD], value[:, HD:])
                product = dot_last(weight, jnp.concatenate(rows, axis=0))
                out_refs[s][v, p] = product.astype(jnp.bfloat16)


def score_kernel(count, group, width, me_ref, q_ref, k_ref, *refs):
    others, (e_ref, stat_ref) = refs[: count - 1], refs[count - 1 :]
    first = (me_ref[0] & (group - 1)) * width
    items, rows, _ = q_ref.shape

    def one(i, carry):
        for p in range(width // PAIR):
            own = pl.ds(pl.multiple_of(first + p * PAIR, PAIR), PAIR)
            here = slice(p * PAIR, (p + 1) * PAIR)
            query = jnp.concatenate([q_ref[i, :, own]] + [r[i, :, here] for r in others], axis=0)
            keys = []
            for s in range(group):
                if s == 0:
                    key = k_ref[i, :, own]
                else:
                    key = others[s - 1][i, :, width + p * PAIR : width + (p + 1) * PAIR]
                keys += side_by_side(key[:, :HD], key[:, HD:])
            scores = dot_last(jnp.concatenate(keys, axis=0), query) * (HD ** (-0.5))
            for h in range(2):
                places = [slice((2 * s + h) * rows, (2 * s + h + 1) * rows) for s in range(group)]
                top = functools.reduce(jnp.maximum, [scores[place] for place in places])
                top = jnp.max(top, axis=0, keepdims=True)
                total = None
                for place in places:
                    exponent = jnp.exp(scores[place] - top)
                    e_ref[i, p, place, :] = exponent
                    total = exponent if total is None else total + exponent
                stat_ref[i, 0, 2 * p + h : 2 * p + h + 1, :] = top
                stat_ref[i, 1, 2 * p + h : 2 * p + h + 1, :] = jnp.sum(
                    total, axis=0, keepdims=True
                )
        return carry

    lax.fori_loop(0, items, one, 0)


def attend_kernel(count, group, scale_ref, skip_ref, e_ref, stat_ref, far_ref, *refs):
    vw_refs, out_ref, scratch = refs[:group], refs[group], refs[group + 1]
    videos, pairs = vw_refs[0].shape[:2]
    rows = e_ref.shape[2] // (2 * group)
    length = rows * count
    half = 2 * rows

    def one(v, carry):
        sums = []
        for way in range(2):
            i = 2 * v + way
            far_top = pltpu.roll(far_ref[i, 0], length // 2, 1)
            far_total = pltpu.roll(far_ref[i, 1], length // 2, 1)
            top = jnp.maximum(stat_ref[i, 0], far_top)
            near = jnp.exp(stat_ref[i, 0] - top)
            total = stat_ref[i, 1] * near + far_total * jnp.exp(far_top - top)
            factor = near / total
            acc = None
            for p in range(pairs):
                weights = []
                values = []
                for s in range(group):
                    for h in range(2):
                        place = slice((2 * s + h) * rows, (2 * s + h + 1) * rows)
                        scaled = e_ref[i, p, place, :] * factor[2 * p + h : 2 * p + h + 1]
                        weights.append(scaled.astype(jnp.bfloat16))
                    values.append(vw_refs[s][v, p][:, way * half : (way + 1) * half])
                term = jnp.dot(
                    jnp.concatenate(values, axis=1),
                    jnp.concatenate(weights, axis=0),
                    preferred_element_type=jnp.float32,
                )
                acc = term if acc is None else acc + term
            sums.append(acc)
        conditional, unconditional = sums
        guided = unconditional + scale_ref[0] * (conditional - unconditional)
        guided = jnp.where(skip_ref[v] == 1, conditional, guided)
        scratch[...] = jnp.concatenate([guided, guided], axis=0).T
        even = scratch[pl.ds(0, length // 2, stride=2), :]
        odd = scratch[pl.ds(1, length // 2, stride=2), :]
        column = lax.broadcasted_iota(jnp.int32, even.shape, 1)
        both = jnp.where(column < CH, even, odd)
        for s in range(count):
            out_ref[s, v] = both[s * rows // 2 : (s + 1) * rows // 2]
        return carry

    lax.fori_loop(0, videos, one, 0)


def call(kernel, outs, specs, name, scratch=(), flops=0, moved=0):
    return pl.pallas_call(
        kernel,
        out_shape=outs,
        in_specs=specs,
        out_specs=jax.tree.map(lambda _: VMEM, outs),
        scratch_shapes=scratch,
        name=name,
        compiler_params=pltpu.CompilerParams(vmem_limit_bytes=16 << 20),
        cost_estimate=pl.CostEstimate(flops=flops, bytes_accessed=moved, transcendentals=0),
    )


def on_device(count, latent, queries, keys, values, head_weight, step_index, skip_flags):
    section_index = lax.axis_index("section")
    me = lax.axis_index("sp")[None]
    _, videos, _, rows, feature_all = queries.shape
    items = videos * 2
    group = count // 2
    width = feature_all // group
    heads = width // HD
    length = rows * count
    query = queries[0].reshape(items, rows, feature_all)
    key = keys[0].reshape(items, rows, feature_all)
    value = values[0].reshape(items, rows, feature_all)

    def exchange(array, s):
        return lax.ppermute(array, "sp", [(i, i ^ s) for i in range(count)])

    def shape(*dims, dtype=jnp.bfloat16):
        return jax.ShapeDtypeStruct(dims, dtype)

    pack = call(
        functools.partial(pack_kernel, count, group, width),
        [shape(items, rows, (2 if s < group else 1) * width) for s in range(1, count)],
        [SMEM, VMEM, VMEM],
        "pack",
        moved=8 * items * rows * feature_all,
    )
    packed = pack(me, query, key)
    arrived = [exchange(packed[s - 1], s) for s in range(1, count)]

    project = call(
        functools.partial(project_kernel, group, width),
        [shape(videos, heads // 2, CH, 4 * rows)] * group,
        [SMEM, VMEM, VMEM],
        "project",
        flops=8 * items * rows * feature_all * CH,
        moved=3 * items * rows * feature_all,
    )
    projected = project(me, value, head_weight[0])
    projected = [projected[0]] + [exchange(projected[s], s) for s in range(1, group)]

    score = call(
        functools.partial(score_kernel, count, group, width),
        [
            shape(items, heads // 2, 2 * group * rows, length, dtype=jnp.float32),
            shape(items, 2, heads, length, dtype=jnp.float32),
        ],
        [SMEM] + [VMEM] * (count + 1),
        "score",
        flops=2 * items * heads * length * length * HD * 4,
        moved=8 * items * rows * feature_all,
    )
    exponents, near = score(me, query, key, *arrived)
    far = exchange(near, group)

    guidance = jnp.where(section_index == 0, jnp.float32(high_guidance), jnp.float32(low_guidance))
    skipping = jnp.where(section_index == 1, skip_flags, 0)
    attend = call(
        functools.partial(attend_kernel, count, group),
        shape(count, videos, rows // 2, 2 * CH, dtype=jnp.float32),
        [SMEM, SMEM] + [VMEM] * (group + 3),
        "attend",
        scratch=[pltpu.VMEM((length, 2 * CH), jnp.float32)],
        flops=2 * items * heads * length * length * HD * 4,
        moved=4 * items * rows * feature_all,
    )
    shares = attend(guidance[None], skipping, exponents, near, far, *projected)
    guided = shares[0]
    for s in range(1, count):
        guided = guided + exchange(shares[s], s)

    step_now = step_index[0]
    step_size = noise_level(step_now + 1) - noise_level(step_now)
    updated = latent[0] + step_size[:, None, None] * guided
    finish_mark = jnp.where(
        (section_index == 0) & (step_now + 1 == SWITCH), jnp.float32(1.0), jnp.float32(0.0)
    )
    arrived_mark = lax.ppermute(finish_mark, "section", [(0, 1)])
    arrived = lax.ppermute(updated, "section", [(0, 1)])
    taking = (section_index == 1) & (arrived_mark > 0.5)
    next_latent = jnp.where(taking[:, None, None], arrived, updated)
    return (guided[None], next_latent[None])


def solution(mesh):
    placed = (
        P("section", ("groups", "blk"), "sp", None),
        P("section", ("groups", "blk"), None, "sp", None),
        P("section", ("groups", "blk"), None, "sp", None),
        P("section", ("groups", "blk"), None, "sp", None),
        P("section", None, None),
        P("section", ("groups", "blk")),
        P(("groups", "blk")),
    )
    return jax.shard_map(
        functools.partial(on_device, mesh.shape["sp"]),
        mesh=mesh,
        in_specs=placed,
        out_specs=(
            P("section", ("groups", "blk"), "sp", None),
            P("section", ("groups", "blk"), "sp", None),
        ),
        check_vma=False,
    )
```

```python
import functools

import jax
import jax.numpy as jnp
from jax import lax
from jax.experimental import pallas as pl
from jax.experimental.pallas import tpu as pltpu
from jax.sharding import PartitionSpec as P

HD = 128
CH = 64
STEPS = 40
SWITCH = 25


noise_shift = 12.0
high_guidance = 4.0
low_guidance = 3.0

VMEM = pl.BlockSpec(memory_space=pltpu.VMEM)
SMEM = pl.BlockSpec(memory_space=pltpu.SMEM)
HBM = pl.BlockSpec(memory_space=pltpu.HBM)
PAIR = 2 * HD


def noise_level(step_now):
    fraction = 1.0 - step_now.astype(jnp.float32) / STEPS
    return noise_shift * fraction / (1.0 + (noise_shift - 1.0) * fraction)


def dot_last(left, right):
    return lax.dot_general(
        left, right, (((1,), (1,)), ((), ())), preferred_element_type=jnp.float32
    )


def side_by_side(first, second):
    zero = jnp.zeros_like(first)
    return [
        jnp.concatenate([first, zero], axis=1),
        jnp.concatenate([zero, second], axis=1),
    ]


def pack_kernel(first, group, width, shifts, me_ref, q_ref, *refs):
    out_refs, sems = refs[:-1], refs[-1]
    copies = []
    for n, (s, out_ref) in enumerate(zip(shifts, out_refs)):
        start = pl.multiple_of(((me_ref[0] ^ s) & (group - 1)) * width, width)
        for i in range(out_ref.shape[0]):
            copies.append(
                pltpu.make_async_copy(
                    q_ref.at[first + i, :, pl.ds(start, width)], out_ref.at[i], sems.at[n, i]
                )
            )
    for copy in copies:
        copy.start()
    for copy in copies:
        copy.wait()


def pack_near_kernel(first, group, width, me_ref, q_ref, k_ref, *refs):
    out_refs, sems = refs[:-1], refs[-1]
    copies = []
    for s in range(1, group):
        start = pl.multiple_of(((me_ref[0] ^ s) & (group - 1)) * width, width)
        for n, ref in enumerate([q_ref, k_ref]):
            for i in range(out_refs[0].shape[0]):
                copies.append(
                    pltpu.make_async_copy(
                        ref.at[first + i, :, pl.ds(start, width)],
                        out_refs[s - 1].at[i, :, pl.ds(n * width, width)],
                        sems.at[s - 1, n, i],
                    )
                )
    for copy in copies:
        copy.start()
    for copy in copies:
        copy.wait()


def project_kernel(first, group, width, me_ref, v_ref, w_ref, *out_refs):
    me = me_ref[0]
    videos = out_refs[0].shape[0]
    for s in range(group):
        lane = ((me ^ s) & (group - 1)) * width
        for p in range(width // PAIR):
            start = pl.multiple_of(lane + p * PAIR, PAIR)
            weight = w_ref[:, pl.ds(start, PAIR)]
            for v in range(videos):
                rows = []
                for way in range(2):
                    value = v_ref[2 * (first + v) + way, :, pl.ds(start, PAIR)]
                    rows += side_by_side(value[:, :HD], value[:, HD:])
                product = dot_last(weight, jnp.concatenate(rows, axis=0))
                out_refs[s][v, p] = product.astype(jnp.bfloat16)


def score_kernel(first, count, group, width, me_ref, q_ref, k_ref, *refs):
    others, outs = refs[: count - 1], refs[count - 1 :]
    whole = group == count
    lane = (me_ref[0] & (group - 1)) * width
    rows = q_ref.shape[1]
    items = outs[0].shape[0]

    def one(i, carry):
        for p in range(width // PAIR):
            own = pl.ds(pl.multiple_of(lane + p * PAIR, PAIR), PAIR)
            here = slice(p * PAIR, (p + 1) * PAIR)
            query = jnp.concatenate(
                [q_ref[2 * first + i, :, own]] + [r[i, :, here] for r in others], axis=0
            )
            keys = []
            for s in range(group):
                if s == 0:
                    key = k_ref[2 * first + i, :, own]
                else:
                    key = others[s - 1][i, :, width + p * PAIR : width + (p + 1) * PAIR]
                keys += side_by_side(key[:, :HD], key[:, HD:])
            scores = dot_last(jnp.concatenate(keys, axis=0), query) * (HD ** (-0.5))
            for h in range(2):
                places = [slice((2 * s + h) * rows, (2 * s + h + 1) * rows) for s in range(group)]
                top = functools.reduce(jnp.maximum, [scores[place] for place in places])
                top = jnp.max(top, axis=0, keepdims=True)
                exponents = [jnp.exp(scores[place] - top) for place in places]
                total = jnp.sum(
                    functools.reduce(jnp.add, exponents), axis=0, keepdims=True
                )
                if whole:
                    share = 1.0 / total
                    exponents = [(e * share).astype(jnp.bfloat16) for e in exponents]
                else:
                    outs[1][i, 0, 2 * p + h : 2 * p + h + 1, :] = top
                    outs[1][i, 1, 2 * p + h : 2 * p + h + 1, :] = total
                for place, e in zip(places, exponents):
                    outs[0][i, p, place, :] = e
        return carry

    lax.fori_loop(0, items, one, 0)


def attend_kernel(first, count, group, keep, scale_ref, skip_ref, *refs):
    scratch, refs = refs[-1], refs[:-1]
    whole = group == count
    e_ref, refs = refs[0], refs[1:]
    if not whole:
        (stat_ref, far_ref), refs = refs[:2], refs[2:]
    vw_refs, refs = refs[:group], refs[group:]
    before_refs, out_refs = (refs[:count] if keep else ()), refs[-count:]
    items, pairs = e_ref.shape[:2]
    rows = e_ref.shape[2] // (2 * group)
    length = rows * count
    half = 2 * rows
    offset = first if before_refs else 0

    def one(v, carry):
        sums = []
        for way in range(2):
            i = 2 * v + way
            if not whole:
                far_top = pltpu.roll(far_ref[i, 0], length // 2, 1)
                far_total = pltpu.roll(far_ref[i, 1], length // 2, 1)
                top = jnp.maximum(stat_ref[i, 0], far_top)
                near = jnp.exp(stat_ref[i, 0] - top)
                factor = near / (stat_ref[i, 1] * near + far_total * jnp.exp(far_top - top))
            acc = None
            for p in range(pairs):
                weights = []
                values = []
                for s in range(group):
                    for h in range(2):
                        e = e_ref[i, p, (2 * s + h) * rows : (2 * s + h + 1) * rows, :]
                        if not whole:
                            e = (e * factor[2 * p + h : 2 * p + h + 1]).astype(jnp.bfloat16)
                        weights.append(e)
                    values.append(vw_refs[s][v, p][:, way * half : (way + 1) * half])
                term = jnp.dot(
                    jnp.concatenate(values, axis=1),
                    jnp.concatenate(weights, axis=0),
                    preferred_element_type=jnp.float32,
                )
                acc = term if acc is None else acc + term
            sums.append(acc)
        conditional, unconditional = sums
        guided = unconditional + scale_ref[0] * (conditional - unconditional)
        guided = jnp.where(skip_ref[first + v] == 1, conditional, guided)
        scratch[...] = jnp.concatenate([guided, guided], axis=0).T
        even = scratch[pl.ds(0, length // 2, stride=2), :]
        odd = scratch[pl.ds(1, length // 2, stride=2), :]
        column = lax.broadcasted_iota(jnp.int32, even.shape, 1)
        both = jnp.where(column < CH, even, odd)
        for s in range(count):
            out_refs[s][offset + v] = both[s * rows // 2 : (s + 1) * rows // 2]
        return carry

    lax.fori_loop(0, items // 2, one, 0)
    for before_ref, out_ref in zip(before_refs, out_refs):
        out_ref[0:first] = before_ref[...]


def call(kernel, outs, specs, name, scratch=(), flops=0, moved=0, space=VMEM, limit=16 << 20):
    return pl.pallas_call(
        kernel,
        out_shape=outs,
        in_specs=specs,
        out_specs=space if isinstance(space, list) else jax.tree.map(lambda _: space, outs),
        scratch_shapes=scratch,
        name=name,
        compiler_params=pltpu.CompilerParams(vmem_limit_bytes=limit),
        cost_estimate=pl.CostEstimate(flops=flops, bytes_accessed=moved, transcendentals=0),
    )


def after(array, *others):
    return lax.optimization_barrier((array, *others))[0]


def shape(*dims, dtype=jnp.bfloat16):
    return jax.ShapeDtypeStruct(dims, dtype)


def on_device(count, latent, queries, keys, values, head_weight, step_index, skip_flags):
    section_index = lax.axis_index("section")
    me = lax.axis_index("sp")[None]
    _, videos, _, rows, feature_all = queries.shape
    items = videos * 2
    length = rows * count
    query = queries[0].reshape(items, rows, feature_all)
    key = keys[0].reshape(items, rows, feature_all)
    value = values[0].reshape(items, rows, feature_all)
    late = max(1, videos // 3)
    early = videos - late

    def exchange(array, s):
        return lax.ppermute(array, "sp", [(i, i ^ s) for i in range(count)])

    def pack(me, first, many, group, shifts):
        width = feature_all // group
        return call(
            functools.partial(pack_kernel, 2 * first, group, width, shifts),
            [shape(2 * many, rows, width)] * len(shifts),
            [SMEM, HBM],
            "pack",
            scratch=[pltpu.SemaphoreType.DMA((len(shifts), 2 * many))],
            moved=8 * many * rows * width * len(shifts),
            limit=None,
        )(me, query)

    def pack_near(me, first, many, group):
        width = feature_all // group
        return call(
            functools.partial(pack_near_kernel, 2 * first, group, width),
            [shape(2 * many, rows, 2 * width)] * (group - 1),
            [SMEM, HBM, HBM],
            "pack_near",
            scratch=[pltpu.SemaphoreType.DMA((group - 1, 2, 2 * many))],
            moved=16 * many * rows * width * (group - 1),
            limit=None,
        )(me, query, key)

    def project(me, first, many, group):
        width = feature_all // group
        return call(
            functools.partial(project_kernel, first, group, width),
            [shape(many, width // PAIR, CH, 4 * rows)] * group,
            [SMEM, VMEM, VMEM],
            "project",
            flops=16 * many * rows * feature_all * CH,
            moved=6 * many * rows * feature_all,
        )(me, value, head_weight[0])

    def score(me, first, many, group, arrived):
        width = feature_all // group
        heads = width // HD
        dims = (2 * many, heads // 2, 2 * group * rows, length)
        if group == count:
            outs = [shape(*dims)]
        else:
            outs = [
                shape(*dims, dtype=jnp.float32),
                shape(2 * many, 2, heads, length, dtype=jnp.float32),
            ]
        return call(
            functools.partial(score_kernel, first, count, group, width),
            outs,
            [SMEM] + [VMEM] * (count + 1),
            "score",
            flops=16 * many * heads * length * length * HD,
            moved=16 * many * rows * feature_all,
        )(me, query, key, *[arrived[s] for s in range(1, count)])

    guidance = jnp.where(section_index == 0, jnp.float32(high_guidance), jnp.float32(low_guidance))
    skipping = jnp.where(section_index == 1, skip_flags, 0)

    def attend(first, group, weights, projected, before=()):
        many = projected[0].shape[0]
        total = first + many
        return call(
            functools.partial(attend_kernel, first, count, group, bool(before)),
            [shape(total, rows // 2, 2 * CH, dtype=jnp.float32)] * count,
            [SMEM, SMEM] + [VMEM] * (len(weights) + group + len(before)),
            "attend",
            scratch=[pltpu.VMEM((length, 2 * CH), jnp.float32)],
            flops=16 * many * feature_all * length * HD,
            moved=8 * many * rows * feature_all,
        )(guidance[None], skipping, *weights, *projected, *before)

    half = count // 2
    step_now = step_index[0]
    finish_mark = jnp.where(
        (section_index == 0) & (step_now + 1 == SWITCH), jnp.float32(1.0), jnp.float32(0.0)
    )

    far_shifts = list(range(count - 1, half - 1, -1))

    def send_far(first, many):
        packed = pack(me, first, many, half, far_shifts)
        return {s: exchange(array, s) for s, array in zip(far_shifts, packed)}

    def send_near(first, many, gate=()):
        packed = pack_near(me, first, many, half)
        return {s: exchange(after(array, *gate), s) for s, array in enumerate(packed, 1)}

    def send_values(first, many, gate=()):
        sent = project(me, first, many, half)
        return [sent[0]] + [exchange(after(sent[s], *gate), s) for s in range(1, half)]

    arrived = send_far(0, early)
    arrived.update(send_near(0, early))
    late_arrived = send_far(early, late)
    late_arrived.update(send_near(early, late, [arrived[half]]))
    values_here = send_values(0, early, [arrived[count - 1]])
    late_values = send_values(early, late, [arrived[1]])

    arrived_mark = lax.ppermute(finish_mark, "section", [(0, 1)])
    exponents, near = score(after(me, arrived_mark), 0, early, half, arrived)
    far = exchange(near, half)
    shares = attend(0, half, [exponents, near, far], values_here)

    exponents, near = score(me, early, late, half, late_arrived)
    far = exchange(near, half)
    shares = attend(early, half, [exponents, near, far], late_values, shares)

    guided = shares[0]
    for s in range(1, count):
        guided = guided + exchange(shares[s], s)
    step_size = noise_level(step_now + 1) - noise_level(step_now)
    updated = latent[0] + step_size[:, None, None] * guided
    taken = lax.ppermute(updated, "section", [(0, 1)])
    taking = (section_index == 1) & (arrived_mark > 0.5)
    next_latent = jnp.where(taking[:, None, None], taken, updated)
    return (guided[None], next_latent[None])


def solution(mesh):
    placed = (
        P("section", ("groups", "blk"), "sp", None),
        P("section", ("groups", "blk"), None, "sp", None),
        P("section", ("groups", "blk"), None, "sp", None),
        P("section", ("groups", "blk"), None, "sp", None),
        P("section", None, None),
        P("section", ("groups", "blk")),
        P(("groups", "blk")),
    )
    return jax.shard_map(
        functools.partial(on_device, mesh.shape["sp"]),
        mesh=mesh,
        in_specs=placed,
        out_specs=(
            P("section", ("groups", "blk"), "sp", None),
            P("section", ("groups", "blk"), "sp", None),
        ),
        check_vma=False,
    )
```

```python
import functools

import jax
import jax.numpy as jnp
from jax import lax
from jax.experimental import pallas as pl
from jax.experimental.pallas import tpu as pltpu
from jax.sharding import PartitionSpec as P

HD = 128
CH = 64
STEPS = 40
SWITCH = 25


noise_shift = 12.0
high_guidance = 4.0
low_guidance = 3.0

VMEM = pl.BlockSpec(memory_space=pltpu.VMEM)
SMEM = pl.BlockSpec(memory_space=pltpu.SMEM)
HBM = pl.BlockSpec(memory_space=pltpu.HBM)
PAIR = 2 * HD


def noise_level(step_now):
    fraction = 1.0 - step_now.astype(jnp.float32) / STEPS
    return noise_shift * fraction / (1.0 + (noise_shift - 1.0) * fraction)


def dot_last(left, right):
    return lax.dot_general(
        left, right, (((1,), (1,)), ((), ())), preferred_element_type=jnp.float32
    )


def side_by_side(first, second):
    zero = jnp.zeros_like(first)
    return [
        jnp.concatenate([first, zero], axis=1),
        jnp.concatenate([zero, second], axis=1),
    ]


def through(moves, staged, sems_in, sems_out):
    inward = [
        pltpu.make_async_copy(source, staged.at[n], sems_in.at[n])
        for n, (source, _) in enumerate(moves)
    ]
    outward = [
        pltpu.make_async_copy(staged.at[n], target, sems_out.at[n])
        for n, (_, target) in enumerate(moves)
    ]
    for copy in inward:
        copy.start()
    for before, copy in zip(inward, outward):
        before.wait()
        copy.start()
    for copy in outward:
        copy.wait()


def pack_kernel(first, group, width, me_ref, q_ref, k_ref, *refs):
    out_refs, scratch = refs[:-3], refs[-3:]
    moves = []
    for s, out_ref in enumerate(out_refs, 1):
        start = pl.multiple_of(((me_ref[0] ^ s) & (group - 1)) * width, width)
        for n, ref in enumerate([q_ref, k_ref] if s < group else [q_ref]):
            for i in range(out_ref.shape[0]):
                moves.append(
                    (
                        ref.at[first + i, :, pl.ds(start, width)],
                        out_ref.at[i, :, pl.ds(n * width, width)],
                    )
                )
    through(moves, *scratch)


def project_kernel(first, group, width, me_ref, v_ref, w_ref, *out_refs):
    me = me_ref[0]
    videos = out_refs[0].shape[0]
    for s in range(group):
        lane = ((me ^ s) & (group - 1)) * width
        for p in range(width // PAIR):
            start = pl.multiple_of(lane + p * PAIR, PAIR)
            weight = w_ref[:, pl.ds(start, PAIR)]
            for v in range(videos):
                rows = []
                for way in range(2):
                    value = v_ref[2 * (first + v) + way, :, pl.ds(start, PAIR)]
                    rows += side_by_side(value[:, :HD], value[:, HD:])
                product = dot_last(weight, jnp.concatenate(rows, axis=0)).astype(jnp.bfloat16)
                half = product.shape[1] // 2
                for way in range(2):
                    out_refs[s][v, way, p // 2, :, (p % 2) * half : (p % 2 + 1) * half] = product[
                        :, way * half : (way + 1) * half
                    ]


def score_kernel(first, count, group, width, me_ref, q_ref, k_ref, *refs):
    others, outs = refs[: count - 1], refs[count - 1 :]
    whole = group == count
    lane = (me_ref[0] & (group - 1)) * width
    rows = q_ref.shape[1]
    items = outs[0].shape[0]

    def one(i, carry):
        for p in range(width // PAIR):
            own = pl.ds(pl.multiple_of(lane + p * PAIR, PAIR), PAIR)
            here = slice(p * PAIR, (p + 1) * PAIR)
            query = jnp.concatenate(
                [q_ref[2 * first + i, :, own]] + [r[i, :, here] for r in others], axis=0
            )
            keys = []
            for s in range(group):
                if s == 0:
                    key = k_ref[2 * first + i, :, own]
                else:
                    key = others[s - 1][i, :, width + p * PAIR : width + (p + 1) * PAIR]
                keys += side_by_side(key[:, :HD], key[:, HD:])
            scores = dot_last(jnp.concatenate(keys, axis=0), query) * (HD ** (-0.5))
            for h in range(2):
                places = [slice((2 * s + h) * rows, (2 * s + h + 1) * rows) for s in range(group)]
                top = functools.reduce(jnp.maximum, [scores[place] for place in places])
                top = jnp.max(top, axis=0, keepdims=True)
                exponents = [jnp.exp(scores[place] - top) for place in places]
                total = jnp.sum(
                    functools.reduce(jnp.add, exponents), axis=0, keepdims=True
                )
                if whole:
                    share = 1.0 / total
                    exponents = [(e * share).astype(jnp.bfloat16) for e in exponents]
                else:
                    outs[1][i, 2 * p + h : 2 * p + h + 1, :] = top
                    outs[2][i, 2 * p + h : 2 * p + h + 1, :] = top + jnp.log(total)
                row = (2 * (p % 2) + h) * rows
                for s, e in enumerate(exponents):
                    outs[0][i, p // 2, s, row : row + rows, :] = e
        return carry

    lax.fori_loop(0, items, one, 0)


def factors(i, top_ref, near_ref, far_ref):
    far = pltpu.roll(far_ref[i], far_ref.shape[2] // 2, 1)
    near = near_ref[i]
    most = jnp.maximum(near, far)
    return jnp.exp(top_ref[i] - most - jnp.log(jnp.exp(near - most) + jnp.exp(far - most)))


def weigh(i, group, e_ref, top_ref, near_ref, far_ref):
    factor = factors(i, top_ref, near_ref, far_ref)
    rows = e_ref.shape[3] // 4
    parts = []
    for q in range(e_ref.shape[1]):
        for s in range(group):
            for h in range(4):
                e = e_ref[i, q, s, h * rows : (h + 1) * rows, :]
                parts.append((e * factor[4 * q + h : 4 * q + h + 1]).astype(jnp.bfloat16))
    return jnp.concatenate(parts, axis=0)


def weigh_kernel(group, e_ref, top_ref, near_ref, far_ref, out_ref):
    def one(i, carry):
        out_ref[i] = weigh(i, group, e_ref, top_ref, near_ref, far_ref)
        return carry

    lax.fori_loop(0, e_ref.shape[0], one, 0)


def attend_kernel(first, count, group, parts, scale_ref, skip_ref, *refs):
    weight_refs, refs = refs[:parts], refs[parts:]
    vw_refs, refs = refs[:group], refs[group:]
    before_refs, out_refs, scratch = refs[: -count - 1], refs[-count - 1 : -1], refs[-1]
    items = weight_refs[0].shape[0]
    quads, _, columns = vw_refs[0].shape[2:]
    rows = columns // 4
    length = rows * count
    offset = first if before_refs else 0

    def one(v, carry):
        sums = []
        for way in range(2):
            i = 2 * v + way
            if parts > 1:
                weights = weigh(i, group, *weight_refs)
            else:
                weights = weight_refs[0][i]
            values = [r[v, way, q] for q in range(quads) for r in vw_refs]
            sums.append(
                jnp.dot(
                    jnp.concatenate(values, axis=1), weights, preferred_element_type=jnp.float32
                )
            )
        conditional, unconditional = sums
        guided = unconditional + scale_ref[0] * (conditional - unconditional)
        guided = jnp.where(skip_ref[first + v] == 1, conditional, guided)
        scratch[...] = jnp.concatenate([guided, guided], axis=0).T
        even = scratch[pl.ds(0, length // 2, stride=2), :]
        odd = scratch[pl.ds(1, length // 2, stride=2), :]
        column = lax.broadcasted_iota(jnp.int32, even.shape, 1)
        both = jnp.where(column < CH, even, odd)
        for s in range(count):
            out_refs[s][offset + v] = both[s * rows // 2 : (s + 1) * rows // 2]
        return carry

    lax.fori_loop(0, items // 2, one, 0)
    for before_ref, out_ref in zip(before_refs, out_refs):
        out_ref[0:first] = before_ref[...]


def call(kernel, outs, specs, name, scratch=(), flops=0, moved=0, space=VMEM, limit=16 << 20):
    return pl.pallas_call(
        kernel,
        out_shape=outs,
        in_specs=specs,
        out_specs=space if isinstance(space, list) else jax.tree.map(lambda _: space, outs),
        scratch_shapes=scratch,
        name=name,
        compiler_params=pltpu.CompilerParams(vmem_limit_bytes=limit),
        cost_estimate=pl.CostEstimate(flops=flops, bytes_accessed=moved, transcendentals=0),
    )


def after(array, *others):
    return lax.optimization_barrier((array, *others))[0]


def shape(*dims, dtype=jnp.bfloat16):
    return jax.ShapeDtypeStruct(dims, dtype)


def on_device(count, latent, queries, keys, values, head_weight, step_index, skip_flags):
    section_index = lax.axis_index("section")
    me = lax.axis_index("sp")[None]
    _, videos, _, rows, feature_all = queries.shape
    items = videos * 2
    length = rows * count
    query = queries[0].reshape(items, rows, feature_all)
    key = keys[0].reshape(items, rows, feature_all)
    value = values[0].reshape(items, rows, feature_all)
    late = max(1, videos // 3)
    early = videos - late

    def exchange(array, s):
        return lax.ppermute(array, "sp", [(i, i ^ s) for i in range(count)])

    def staging(number, width):
        return [
            pltpu.VMEM((number, rows, width), jnp.bfloat16),
            pltpu.SemaphoreType.DMA((number,)),
            pltpu.SemaphoreType.DMA((number,)),
        ]

    def pack(me, first, many, group):
        width = feature_all // group
        wide = [(2 if s < group else 1) * width for s in range(1, count)]
        return call(
            functools.partial(pack_kernel, 2 * first, group, width),
            [shape(2 * many, rows, w) for w in wide],
            [SMEM, HBM, HBM],
            "pack",
            scratch=staging(2 * many * (count + group - 2), width),
            moved=8 * many * rows * sum(wide),
            space=HBM,
            limit=None,
        )(me, query, key)

    def project(me, first, many, group):
        width = feature_all // group
        return call(
            functools.partial(project_kernel, first, group, width),
            [shape(many, 2, width // (2 * PAIR), CH, 4 * rows)] * group,
            [SMEM, VMEM, VMEM],
            "project",
            flops=16 * many * rows * feature_all * CH,
            moved=6 * many * rows * feature_all,
        )(me, value, head_weight[0])

    def score(me, first, many, group, arrived):
        width = feature_all // group
        heads = width // HD
        dims = (2 * many, heads // 4, group, 4 * rows, length)
        if group == count:
            outs = [shape(*dims)]
        else:
            outs = [
                shape(*dims, dtype=jnp.float32),
                shape(2 * many, heads, length, dtype=jnp.float32),
                shape(2 * many, heads, length, dtype=jnp.float32),
            ]
        return call(
            functools.partial(score_kernel, first, count, group, width),
            outs,
            [SMEM] + [VMEM] * (count + 1),
            "score",
            flops=16 * many * heads * length * length * HD,
            moved=16 * many * rows * feature_all,
        )(me, query, key, *[arrived[s] for s in range(1, count)])

    guidance = jnp.where(section_index == 0, jnp.float32(high_guidance), jnp.float32(low_guidance))
    skipping = jnp.where(section_index == 1, skip_flags, 0)

    def attend(first, many, group, weights, projected, before=()):
        total = first + many
        return call(
            functools.partial(attend_kernel, first, count, group, len(weights)),
            [shape(total, rows // 2, 2 * CH, dtype=jnp.float32)] * count,
            [SMEM, SMEM] + [VMEM] * (len(weights) + group + len(before)),
            "attend",
            scratch=[pltpu.VMEM((length, 2 * CH), jnp.float32)],
            flops=16 * many * feature_all * length * HD,
            moved=8 * many * rows * feature_all,
        )(guidance[None], skipping, *weights, *projected, *before)

    def weigh_all(exponents, top, near, far):
        return call(
            functools.partial(weigh_kernel, half),
            shape(exponents.shape[0], exponents.size // exponents.shape[0] // length, length),
            [VMEM] * 4,
            "weigh",
            flops=exponents.size,
            moved=6 * exponents.size,
        )(exponents, top, near, far)

    half = count // 2
    step_now = step_index[0]
    step_size = noise_level(step_now + 1) - noise_level(step_now)
    finish_mark = jnp.where(
        (section_index == 0) & (step_now + 1 == SWITCH), jnp.float32(1.0), jnp.float32(0.0)
    )
    far_shifts = list(range(count - 1, half - 1, -1))
    inner = list(range(1, half))
    first = pack(me, 0, early, half)
    second = pack(after(me, first[0]), early, late, half)
    first_values = project(after(me, second[0]), 0, early, half)
    second_values = project(after(me, second[0]), early, late, half)

    arrived = {s: exchange(first[s - 1], s) for s in range(1, count)}
    late_arrived = {s: exchange(second[s - 1], s) for s in far_shifts}
    for s in inner:
        late_arrived[s] = exchange(after(second[s - 1], arrived[half]), s)
    values_here = [first_values[0]] + [
        exchange(after(first_values[s], arrived[half]), s) for s in inner
    ]
    late_values = [second_values[0]] + [
        exchange(after(second_values[s], arrived[1]), s) for s in inner
    ]

    arrived_mark = lax.ppermute(after(finish_mark, arrived[1]), "section", [(0, 1)])
    exponents, top, near = score(after(me, arrived_mark), 0, early, half, arrived)
    weights = weigh_all(exponents, top, near, exchange(near, half))
    shares = attend(0, early, half, [weights], values_here)

    exponents, top, near = score(me, early, late, half, late_arrived)
    far = exchange(near, half)
    shares = attend(early, late, half, [exponents, top, near, far], late_values, shares)

    guided = shares[0]
    for s in range(1, count):
        guided = guided + exchange(shares[s], s)
    updated = latent[0] + step_size[:, None, None] * guided
    taken = lax.ppermute(updated, "section", [(0, 1)])
    taking = (section_index == 1) & (arrived_mark > 0.5)
    next_latent = jnp.where(taking[:, None, None], taken, updated)
    return (guided[None], next_latent[None])


def solution(mesh):
    placed = (
        P("section", ("groups", "blk"), "sp", None),
        P("section", ("groups", "blk"), None, "sp", None),
        P("section", ("groups", "blk"), None, "sp", None),
        P("section", ("groups", "blk"), None, "sp", None),
        P("section", None, None),
        P("section", ("groups", "blk")),
        P(("groups", "blk")),
    )
    return jax.shard_map(
        functools.partial(on_device, mesh.shape["sp"]),
        mesh=mesh,
        in_specs=placed,
        out_specs=(
            P("section", ("groups", "blk"), "sp", None),
            P("section", ("groups", "blk"), "sp", None),
        ),
        check_vma=False,
    )
```

```python
import functools

import jax
import jax.numpy as jnp
from jax import lax
from jax.experimental import pallas as pl
from jax.experimental.pallas import tpu as pltpu
from jax.sharding import PartitionSpec as P

HD = 128
CH = 64
STEPS = 40
SWITCH = 25


noise_shift = 12.0
high_guidance = 4.0
low_guidance = 3.0

VMEM = pl.BlockSpec(memory_space=pltpu.VMEM)
SMEM = pl.BlockSpec(memory_space=pltpu.SMEM)
HBM = pl.BlockSpec(memory_space=pltpu.HBM)
PAIR = 2 * HD


def noise_level(step_now):
    fraction = 1.0 - step_now.astype(jnp.float32) / STEPS
    return noise_shift * fraction / (1.0 + (noise_shift - 1.0) * fraction)


def dot_last(left, right):
    return lax.dot_general(
        left, right, (((1,), (1,)), ((), ())), preferred_element_type=jnp.float32
    )


def side_by_side(first, second):
    zero = jnp.zeros_like(first)
    return [
        jnp.concatenate([first, zero], axis=1),
        jnp.concatenate([zero, second], axis=1),
    ]


def through(moves, staged, sems_in, sems_out):
    inward = [
        pltpu.make_async_copy(source, staged.at[n], sems_in.at[n])
        for n, (source, _) in enumerate(moves)
    ]
    outward = [
        pltpu.make_async_copy(staged.at[n], target, sems_out.at[n])
        for n, (_, target) in enumerate(moves)
    ]
    for copy in inward:
        copy.start()
    for before, copy in zip(inward, outward):
        before.wait()
        copy.start()
    for copy in outward:
        copy.wait()


def pack_kernel(first, group, width, me_ref, q_ref, k_ref, *refs):
    out_refs, scratch = refs[:-3], refs[-3:]
    moves = []
    for s, out_ref in enumerate(out_refs, 1):
        start = pl.multiple_of(((me_ref[0] ^ s) & (group - 1)) * width, width)
        for n, ref in enumerate([q_ref, k_ref] if s < group else [q_ref]):
            for i in range(out_ref.shape[0]):
                moves.append(
                    (
                        ref.at[first + i, :, pl.ds(start, width)],
                        out_ref.at[i, :, pl.ds(n * width, width)],
                    )
                )
    through(moves, *scratch)


def project_kernel(first, group, width, me_ref, v_ref, w_ref, *out_refs):
    me = me_ref[0]
    videos = out_refs[0].shape[0]
    for s in range(group):
        lane = ((me ^ s) & (group - 1)) * width
        for p in range(width // PAIR):
            start = pl.multiple_of(lane + p * PAIR, PAIR)
            weight = w_ref[:, pl.ds(start, PAIR)]
            for v in range(videos):
                rows = []
                for way in range(2):
                    value = v_ref[2 * (first + v) + way, :, pl.ds(start, PAIR)]
                    rows += side_by_side(value[:, :HD], value[:, HD:])
                product = dot_last(weight, jnp.concatenate(rows, axis=0)).astype(jnp.bfloat16)
                half = product.shape[1] // 2
                for way in range(2):
                    out_refs[s][v, way, p // 2, :, (p % 2) * half : (p % 2 + 1) * half] = product[
                        :, way * half : (way + 1) * half
                    ]


def score_kernel(first, count, group, width, me_ref, q_ref, k_ref, *refs):
    others, outs = refs[: count - 1], refs[count - 1 :]
    whole = group == count
    lane = (me_ref[0] & (group - 1)) * width
    rows = q_ref.shape[1]
    items = outs[0].shape[0]

    def one(i, carry):
        for p in range(width // PAIR):
            own = pl.ds(pl.multiple_of(lane + p * PAIR, PAIR), PAIR)
            here = slice(p * PAIR, (p + 1) * PAIR)
            query = jnp.concatenate(
                [q_ref[2 * first + i, :, own]] + [r[i, :, here] for r in others], axis=0
            )
            keys = []
            for s in range(group):
                if s == 0:
                    key = k_ref[2 * first + i, :, own]
                else:
                    key = others[s - 1][i, :, width + p * PAIR : width + (p + 1) * PAIR]
                keys += side_by_side(key[:, :HD], key[:, HD:])
            scores = dot_last(jnp.concatenate(keys, axis=0), query) * (HD ** (-0.5))
            for h in range(2):
                places = [slice((2 * s + h) * rows, (2 * s + h + 1) * rows) for s in range(group)]
                top = functools.reduce(jnp.maximum, [scores[place] for place in places])
                top = jnp.max(top, axis=0, keepdims=True)
                exponents = [jnp.exp(scores[place] - top) for place in places]
                total = jnp.sum(
                    functools.reduce(jnp.add, exponents), axis=0, keepdims=True
                )
                if whole:
                    share = 1.0 / total
                    exponents = [(e * share).astype(jnp.bfloat16) for e in exponents]
                else:
                    outs[1][i, 2 * p + h : 2 * p + h + 1, :] = top
                    outs[2][i, 2 * p + h : 2 * p + h + 1, :] = top + jnp.log(total)
                row = (2 * (p % 2) + h) * rows
                for s, e in enumerate(exponents):
                    outs[0][i, p // 2, s, row : row + rows, :] = e
        return carry

    lax.fori_loop(0, items, one, 0)


def factors(i, top_ref, near_ref, far_ref):
    far = pltpu.roll(far_ref[i], far_ref.shape[2] // 2, 1)
    near = near_ref[i]
    most = jnp.maximum(near, far)
    return jnp.exp(top_ref[i] - most - jnp.log(jnp.exp(near - most) + jnp.exp(far - most)))


def weigh(i, group, e_ref, top_ref, near_ref, far_ref):
    factor = factors(i, top_ref, near_ref, far_ref)
    rows = e_ref.shape[3] // 4
    parts = []
    for q in range(e_ref.shape[1]):
        for s in range(group):
            for h in range(4):
                e = e_ref[i, q, s, h * rows : (h + 1) * rows, :]
                parts.append((e * factor[4 * q + h : 4 * q + h + 1]).astype(jnp.bfloat16))
    return jnp.concatenate(parts, axis=0)


def weigh_kernel(group, e_ref, top_ref, near_ref, far_ref, out_ref):
    def one(i, carry):
        out_ref[i] = weigh(i, group, e_ref, top_ref, near_ref, far_ref)
        return carry

    lax.fori_loop(0, e_ref.shape[0], one, 0)


def attend_kernel(first, count, group, parts, scale_ref, skip_ref, *refs):
    weight_refs, refs = refs[:parts], refs[parts:]
    vw_refs, refs = refs[:group], refs[group:]
    before_refs, out_refs, scratch = refs[: -count - 1], refs[-count - 1 : -1], refs[-1]
    items = weight_refs[0].shape[0]
    quads, _, columns = vw_refs[0].shape[2:]
    rows = columns // 4
    length = rows * count
    offset = first if before_refs else 0

    def one(v, carry):
        sums = []
        for way in range(2):
            i = 2 * v + way
            if parts > 1:
                weights = weigh(i, group, *weight_refs)
            else:
                weights = weight_refs[0][i]
            values = [r[v, way, q] for q in range(quads) for r in vw_refs]
            sums.append(
                jnp.dot(
                    jnp.concatenate(values, axis=1), weights, preferred_element_type=jnp.float32
                )
            )
        conditional, unconditional = sums
        guided = unconditional + scale_ref[0] * (conditional - unconditional)
        guided = jnp.where(skip_ref[first + v] == 1, conditional, guided)
        scratch[...] = jnp.concatenate([guided, guided], axis=0).T
        even = scratch[pl.ds(0, length // 2, stride=2), :]
        odd = scratch[pl.ds(1, length // 2, stride=2), :]
        column = lax.broadcasted_iota(jnp.int32, even.shape, 1)
        both = jnp.where(column < CH, even, odd)
        for s in range(count):
            out_refs[s][offset + v] = both[s * rows // 2 : (s + 1) * rows // 2]
        return carry

    lax.fori_loop(0, items // 2, one, 0)
    for before_ref, out_ref in zip(before_refs, out_refs):
        out_ref[0:first] = before_ref[...]


def call(kernel, outs, specs, name, scratch=(), flops=0, moved=0, space=VMEM, limit=16 << 20):
    return pl.pallas_call(
        kernel,
        out_shape=outs,
        in_specs=specs,
        out_specs=space if isinstance(space, list) else jax.tree.map(lambda _: space, outs),
        scratch_shapes=scratch,
        name=name,
        compiler_params=pltpu.CompilerParams(vmem_limit_bytes=limit),
        cost_estimate=pl.CostEstimate(flops=flops, bytes_accessed=moved, transcendentals=0),
    )


def after(array, *others):
    return lax.optimization_barrier((array, *others))[0]


def shape(*dims, dtype=jnp.bfloat16):
    return jax.ShapeDtypeStruct(dims, dtype)


def on_device(count, latent, queries, keys, values, head_weight, step_index, skip_flags):
    section_index = lax.axis_index("section")
    me = lax.axis_index("sp")[None]
    _, videos, _, rows, feature_all = queries.shape
    items = videos * 2
    length = rows * count
    query = queries[0].reshape(items, rows, feature_all)
    key = keys[0].reshape(items, rows, feature_all)
    value = values[0].reshape(items, rows, feature_all)
    late = max(1, videos // 3)
    early = videos - late

    def exchange(array, s):
        return lax.ppermute(array, "sp", [(i, i ^ s) for i in range(count)])

    def staging(number, width):
        return [
            pltpu.VMEM((number, rows, width), jnp.bfloat16),
            pltpu.SemaphoreType.DMA((number,)),
            pltpu.SemaphoreType.DMA((number,)),
        ]

    def pack(me, first, many, group):
        width = feature_all // group
        wide = [(2 if s < group else 1) * width for s in range(1, count)]
        return call(
            functools.partial(pack_kernel, 2 * first, group, width),
            [shape(2 * many, rows, w) for w in wide],
            [SMEM, HBM, HBM],
            "pack",
            scratch=staging(2 * many * (count + group - 2), width),
            moved=8 * many * rows * sum(wide),
            space=HBM,
            limit=None,
        )(me, query, key)

    def project(me, first, many, group):
        width = feature_all // group
        return call(
            functools.partial(project_kernel, first, group, width),
            [shape(many, 2, width // (2 * PAIR), CH, 4 * rows)] * group,
            [SMEM, VMEM, VMEM],
            "project",
            flops=16 * many * rows * feature_all * CH,
            moved=6 * many * rows * feature_all,
        )(me, value, head_weight[0])

    def score(me, first, many, group, arrived):
        width = feature_all // group
        heads = width // HD
        dims = (2 * many, heads // 4, group, 4 * rows, length)
        if group == count:
            outs = [shape(*dims)]
        else:
            outs = [
                shape(*dims, dtype=jnp.float32),
                shape(2 * many, heads, length, dtype=jnp.float32),
                shape(2 * many, heads, length, dtype=jnp.float32),
            ]
        return call(
            functools.partial(score_kernel, first, count, group, width),
            outs,
            [SMEM] + [VMEM] * (count + 1),
            "score",
            flops=16 * many * heads * length * length * HD,
            moved=16 * many * rows * feature_all,
        )(me, query, key, *[arrived[s] for s in range(1, count)])

    guidance = jnp.where(section_index == 0, jnp.float32(high_guidance), jnp.float32(low_guidance))
    skipping = jnp.where(section_index == 1, skip_flags, 0)

    def attend(first, many, group, weights, projected, before=()):
        total = first + many
        return call(
            functools.partial(attend_kernel, first, count, group, len(weights)),
            [shape(total, rows // 2, 2 * CH, dtype=jnp.float32)] * count,
            [SMEM, SMEM] + [VMEM] * (len(weights) + group + len(before)),
            "attend",
            scratch=[pltpu.VMEM((length, 2 * CH), jnp.float32)],
            flops=16 * many * feature_all * length * HD,
            moved=8 * many * rows * feature_all,
        )(guidance[None], skipping, *weights, *projected, *before)

    def weigh_all(exponents, top, near, far):
        return call(
            functools.partial(weigh_kernel, half),
            shape(exponents.shape[0], exponents.size // exponents.shape[0] // length, length),
            [VMEM] * 4,
            "weigh",
            flops=exponents.size,
            moved=6 * exponents.size,
        )(exponents, top, near, far)

    half = count // 2
    step_now = step_index[0]
    step_size = noise_level(step_now + 1) - noise_level(step_now)
    finish_mark = jnp.where(
        (section_index == 0) & (step_now + 1 == SWITCH), jnp.float32(1.0), jnp.float32(0.0)
    )
    far_shifts = list(range(count - 1, half - 1, -1))
    inner = list(range(1, half))
    first = pack(me, 0, early, half)
    second = pack(after(me, first[0]), early, late, half)
    first_values = project(after(me, second[0]), 0, early, half)
    second_values = project(after(me, second[0]), early, late, half)

    arrived = {s: exchange(first[s - 1], s) for s in range(1, count)}
    late_arrived = {s: exchange(second[s - 1], s) for s in far_shifts}
    for s in inner:
        late_arrived[s] = exchange(after(second[s - 1], arrived[half]), s)
    values_here = [first_values[0]] + [
        exchange(after(first_values[s], arrived[half]), s) for s in inner
    ]
    late_values = [second_values[0]] + [
        exchange(after(second_values[s], arrived[1]), s) for s in inner
    ]

    arrived_mark = lax.ppermute(after(finish_mark, arrived[1]), "section", [(0, 1)])
    exponents, top, near = score(after(me, arrived_mark), 0, early, half, arrived)
    weights = weigh_all(exponents, top, near, exchange(near, half))
    shares = attend(0, early, half, [weights], values_here)

    exponents, top, near = score(me, early, late, half, late_arrived)
    far = exchange(near, half)
    shares = attend(early, late, half, [exponents, top, near, far], late_values, shares)

    parts = [exchange(shares[s], s) for s in range(count - 1, 0, -1)] + [shares[0]]
    guided = functools.reduce(jnp.add, lax.optimization_barrier(parts))
    updated = latent[0] + step_size[:, None, None] * functools.reduce(jnp.add, parts)
    taken = lax.ppermute(updated, "section", [(0, 1)])
    taking = (section_index == 1) & (arrived_mark > 0.5)
    next_latent = jnp.where(taking[:, None, None], taken, updated)
    return (guided[None], next_latent[None])


def solution(mesh):
    placed = (
        P("section", ("groups", "blk"), "sp", None),
        P("section", ("groups", "blk"), None, "sp", None),
        P("section", ("groups", "blk"), None, "sp", None),
        P("section", ("groups", "blk"), None, "sp", None),
        P("section", None, None),
        P("section", ("groups", "blk")),
        P(("groups", "blk")),
    )
    return jax.shard_map(
        functools.partial(on_device, mesh.shape["sp"]),
        mesh=mesh,
        in_specs=placed,
        out_specs=(
            P("section", ("groups", "blk"), "sp", None),
            P("section", ("groups", "blk"), "sp", None),
        ),
        check_vma=False,
    )
```

```python
import functools

import jax
import jax.numpy as jnp
from jax import lax
from jax.experimental import pallas as pl
from jax.experimental.pallas import tpu as pltpu
from jax.sharding import PartitionSpec as P

HD = 128
CH = 64
STEPS = 40
SWITCH = 25


noise_shift = 12.0
high_guidance = 4.0
low_guidance = 3.0

VMEM = pl.BlockSpec(memory_space=pltpu.VMEM)
SMEM = pl.BlockSpec(memory_space=pltpu.SMEM)
HBM = pl.BlockSpec(memory_space=pltpu.HBM)
PAIR = 2 * HD


def noise_level(step_now):
    fraction = 1.0 - step_now.astype(jnp.float32) / STEPS
    return noise_shift * fraction / (1.0 + (noise_shift - 1.0) * fraction)


def dot_last(left, right):
    return lax.dot_general(
        left, right, (((1,), (1,)), ((), ())), preferred_element_type=jnp.float32
    )


def side_by_side(first, second):
    zero = jnp.zeros_like(first)
    return [
        jnp.concatenate([first, zero], axis=1),
        jnp.concatenate([zero, second], axis=1),
    ]


def through(moves, staged, sems_in, sems_out):
    inward = [
        pltpu.make_async_copy(source, staged.at[n], sems_in.at[n])
        for n, (source, _) in enumerate(moves)
    ]
    outward = [
        pltpu.make_async_copy(staged.at[n], target, sems_out.at[n])
        for n, (_, target) in enumerate(moves)
    ]
    for copy in inward:
        copy.start()
    for before, copy in zip(inward, outward):
        before.wait()
        copy.start()
    for copy in outward:
        copy.wait()


def pack_kernel(first, group, width, me_ref, q_ref, k_ref, *refs):
    out_refs, scratch = refs[:-3], refs[-3:]
    moves = []
    for s, out_ref in enumerate(out_refs, 1):
        start = pl.multiple_of(((me_ref[0] ^ s) & (group - 1)) * width, width)
        for n, ref in enumerate([q_ref, k_ref] if s < group else [q_ref]):
            for i in range(0, out_ref.shape[0], 2):
                moves.append(
                    (
                        ref.at[pl.ds(first + i, 2), :, pl.ds(start, width)],
                        out_ref.at[pl.ds(i, 2), :, pl.ds(n * width, width)],
                    )
                )
    through(moves, *scratch)


def project_kernel(first, group, width, me_ref, v_ref, w_ref, *out_refs):
    me = me_ref[0]
    videos = out_refs[0].shape[0]
    for s in range(group):
        lane = ((me ^ s) & (group - 1)) * width
        for p in range(width // PAIR):
            start = pl.multiple_of(lane + p * PAIR, PAIR)
            weight = w_ref[:, pl.ds(start, PAIR)]
            for v in range(videos):
                rows = []
                for way in range(2):
                    value = v_ref[2 * (first + v) + way, :, pl.ds(start, PAIR)]
                    rows += side_by_side(value[:, :HD], value[:, HD:])
                product = dot_last(weight, jnp.concatenate(rows, axis=0)).astype(jnp.bfloat16)
                half = product.shape[1] // 2
                for way in range(2):
                    out_refs[s][v, way, p // 2, :, (p % 2) * half : (p % 2 + 1) * half] = product[
                        :, way * half : (way + 1) * half
                    ]


def score_kernel(first, count, group, width, me_ref, q_ref, k_ref, *refs):
    others, outs = refs[: count - 1], refs[count - 1 :]
    whole = group == count
    lane = (me_ref[0] & (group - 1)) * width
    rows = q_ref.shape[1]
    items = outs[0].shape[0]

    def one(i, carry):
        for p in range(width // PAIR):
            own = pl.ds(pl.multiple_of(lane + p * PAIR, PAIR), PAIR)
            here = slice(p * PAIR, (p + 1) * PAIR)
            query = jnp.concatenate(
                [q_ref[2 * first + i, :, own]] + [r[i, :, here] for r in others], axis=0
            )
            keys = []
            for s in range(group):
                if s == 0:
                    key = k_ref[2 * first + i, :, own]
                else:
                    key = others[s - 1][i, :, width + p * PAIR : width + (p + 1) * PAIR]
                keys += side_by_side(key[:, :HD], key[:, HD:])
            scores = dot_last(jnp.concatenate(keys, axis=0), query) * (HD ** (-0.5))
            for h in range(2):
                places = [slice((2 * s + h) * rows, (2 * s + h + 1) * rows) for s in range(group)]
                top = functools.reduce(jnp.maximum, [scores[place] for place in places])
                top = jnp.max(top, axis=0, keepdims=True)
                exponents = [jnp.exp(scores[place] - top) for place in places]
                total = jnp.sum(
                    functools.reduce(jnp.add, exponents), axis=0, keepdims=True
                )
                if whole:
                    share = 1.0 / total
                    exponents = [(e * share).astype(jnp.bfloat16) for e in exponents]
                else:
                    outs[1][i, 2 * p + h : 2 * p + h + 1, :] = top
                    outs[2][i, 2 * p + h : 2 * p + h + 1, :] = top + jnp.log(total)
                row = (2 * (p % 2) + h) * rows
                for s, e in enumerate(exponents):
                    outs[0][i, p // 2, s, row : row + rows, :] = e
        return carry

    lax.fori_loop(0, items, one, 0)


def factors(i, top_ref, near_ref, far_ref):
    far = pltpu.roll(far_ref[i], far_ref.shape[2] // 2, 1)
    near = near_ref[i]
    most = jnp.maximum(near, far)
    return jnp.exp(top_ref[i] - most - jnp.log(jnp.exp(near - most) + jnp.exp(far - most)))


def weigh(i, group, e_ref, top_ref, near_ref, far_ref):
    factor = factors(i, top_ref, near_ref, far_ref)
    rows = e_ref.shape[3] // 4
    parts = []
    for q in range(e_ref.shape[1]):
        for s in range(group):
            for h in range(4):
                e = e_ref[i, q, s, h * rows : (h + 1) * rows, :]
                parts.append((e * factor[4 * q + h : 4 * q + h + 1]).astype(jnp.bfloat16))
    return jnp.concatenate(parts, axis=0)


def weigh_kernel(group, e_ref, top_ref, near_ref, far_ref, out_ref):
    def one(i, carry):
        out_ref[i] = weigh(i, group, e_ref, top_ref, near_ref, far_ref)
        return carry

    lax.fori_loop(0, e_ref.shape[0], one, 0)


def attend_kernel(first, count, group, parts, scale_ref, skip_ref, *refs):
    weight_refs, refs = refs[:parts], refs[parts:]
    vw_refs, refs = refs[:group], refs[group:]
    before_refs, out_refs, scratch = refs[: -count - 1], refs[-count - 1 : -1], refs[-1]
    items = weight_refs[0].shape[0]
    quads, _, columns = vw_refs[0].shape[2:]
    rows = columns // 4
    length = rows * count
    offset = first if before_refs else 0

    def one(v, carry):
        sums = []
        for way in range(2):
            i = 2 * v + way
            if parts > 1:
                weights = weigh(i, group, *weight_refs)
            else:
                weights = weight_refs[0][i]
            values = [r[v, way, q] for q in range(quads) for r in vw_refs]
            sums.append(
                jnp.dot(
                    jnp.concatenate(values, axis=1), weights, preferred_element_type=jnp.float32
                )
            )
        conditional, unconditional = sums
        guided = unconditional + scale_ref[0] * (conditional - unconditional)
        guided = jnp.where(skip_ref[first + v] == 1, conditional, guided)
        scratch[...] = jnp.concatenate([guided, guided], axis=0).T
        even = scratch[pl.ds(0, length // 2, stride=2), :]
        odd = scratch[pl.ds(1, length // 2, stride=2), :]
        column = lax.broadcasted_iota(jnp.int32, even.shape, 1)
        both = jnp.where(column < CH, even, odd)
        for s in range(count):
            out_refs[s][offset + v] = both[s * rows // 2 : (s + 1) * rows // 2]
        return carry

    lax.fori_loop(0, items // 2, one, 0)
    for before_ref, out_ref in zip(before_refs, out_refs):
        out_ref[0:first] = before_ref[...]


def call(kernel, outs, specs, name, scratch=(), flops=0, moved=0, space=VMEM, limit=16 << 20):
    return pl.pallas_call(
        kernel,
        out_shape=outs,
        in_specs=specs,
        out_specs=space if isinstance(space, list) else jax.tree.map(lambda _: space, outs),
        scratch_shapes=scratch,
        name=name,
        compiler_params=pltpu.CompilerParams(vmem_limit_bytes=limit),
        cost_estimate=pl.CostEstimate(flops=flops, bytes_accessed=moved, transcendentals=0),
    )


def after(array, *others):
    return lax.optimization_barrier((array, *others))[0]


def shape(*dims, dtype=jnp.bfloat16):
    return jax.ShapeDtypeStruct(dims, dtype)


def on_device(count, latent, queries, keys, values, head_weight, step_index, skip_flags):
    section_index = lax.axis_index("section")
    me = lax.axis_index("sp")[None]
    _, videos, _, rows, feature_all = queries.shape
    items = videos * 2
    length = rows * count
    query = queries[0].reshape(items, rows, feature_all)
    key = keys[0].reshape(items, rows, feature_all)
    value = values[0].reshape(items, rows, feature_all)
    late = max(1, videos // 3)
    early = videos - late

    def exchange(array, s):
        return lax.ppermute(array, "sp", [(i, i ^ s) for i in range(count)])

    def staging(number, width):
        return [
            pltpu.VMEM((number, 2, rows, width), jnp.bfloat16),
            pltpu.SemaphoreType.DMA((number,)),
            pltpu.SemaphoreType.DMA((number,)),
        ]

    def pack(me, first, many, group):
        width = feature_all // group
        wide = [(2 if s < group else 1) * width for s in range(1, count)]
        return call(
            functools.partial(pack_kernel, 2 * first, group, width),
            [shape(2 * many, rows, w) for w in wide],
            [SMEM, HBM, HBM],
            "pack",
            scratch=staging(many * (count + group - 2), width),
            moved=8 * many * rows * sum(wide),
            space=HBM,
            limit=None,
        )(me, query, key)

    def project(me, first, many, group):
        width = feature_all // group
        return call(
            functools.partial(project_kernel, first, group, width),
            [shape(many, 2, width // (2 * PAIR), CH, 4 * rows)] * group,
            [SMEM, VMEM, VMEM],
            "project",
            flops=16 * many * rows * feature_all * CH,
            moved=6 * many * rows * feature_all,
        )(me, value, head_weight[0])

    def score(me, first, many, group, arrived):
        width = feature_all // group
        heads = width // HD
        dims = (2 * many, heads // 4, group, 4 * rows, length)
        if group == count:
            outs = [shape(*dims)]
        else:
            outs = [
                shape(*dims, dtype=jnp.float32),
                shape(2 * many, heads, length, dtype=jnp.float32),
                shape(2 * many, heads, length, dtype=jnp.float32),
            ]
        return call(
            functools.partial(score_kernel, first, count, group, width),
            outs,
            [SMEM] + [VMEM] * (count + 1),
            "score",
            flops=16 * many * heads * length * length * HD,
            moved=16 * many * rows * feature_all,
        )(me, query, key, *[arrived[s] for s in range(1, count)])

    guidance = jnp.where(section_index == 0, jnp.float32(high_guidance), jnp.float32(low_guidance))
    skipping = jnp.where(section_index == 1, skip_flags, 0)

    def attend(first, many, group, weights, projected, before=()):
        total = first + many
        return call(
            functools.partial(attend_kernel, first, count, group, len(weights)),
            [shape(total, rows // 2, 2 * CH, dtype=jnp.float32)] * count,
            [SMEM, SMEM] + [VMEM] * (len(weights) + group + len(before)),
            "attend",
            scratch=[pltpu.VMEM((length, 2 * CH), jnp.float32)],
            flops=16 * many * feature_all * length * HD,
            moved=8 * many * rows * feature_all,
        )(guidance[None], skipping, *weights, *projected, *before)

    def weigh_all(exponents, top, near, far):
        return call(
            functools.partial(weigh_kernel, half),
            shape(exponents.shape[0], exponents.size // exponents.shape[0] // length, length),
            [VMEM] * 4,
            "weigh",
            flops=exponents.size,
            moved=6 * exponents.size,
        )(exponents, top, near, far)

    half = count // 2
    step_now = step_index[0]
    step_size = noise_level(step_now + 1) - noise_level(step_now)
    finish_mark = jnp.where(
        (section_index == 0) & (step_now + 1 == SWITCH), jnp.float32(1.0), jnp.float32(0.0)
    )
    far_shifts = list(range(count - 1, half - 1, -1))
    inner = list(range(1, half))
    first = pack(me, 0, early, half)
    second = pack(after(me, first[0]), early, late, half)
    first_values = project(after(me, second[0]), 0, early, half)
    second_values = project(after(me, second[0]), early, late, half)

    arrived = {s: exchange(first[s - 1], s) for s in range(1, count)}
    late_arrived = {s: exchange(second[s - 1], s) for s in far_shifts}
    for s in inner:
        late_arrived[s] = exchange(after(second[s - 1], arrived[half]), s)
    values_here = [first_values[0]] + [
        exchange(after(first_values[s], arrived[half]), s) for s in inner
    ]
    late_values = [second_values[0]] + [
        exchange(after(second_values[s], arrived[1]), s) for s in inner
    ]

    arrived_mark = lax.ppermute(after(finish_mark, arrived[1]), "section", [(0, 1)])
    exponents, top, near = score(after(me, arrived_mark), 0, early, half, arrived)
    weights = weigh_all(exponents, top, near, exchange(near, half))
    shares = attend(0, early, half, [weights], values_here)

    exponents, top, near = score(me, early, late, half, late_arrived)
    far = exchange(near, half)
    shares = attend(early, late, half, [exponents, top, near, far], late_values, shares)

    parts = [exchange(shares[s], s) for s in [*range(count - 1, half, -1), *range(half - 1, 0, -1), half]] + [shares[0]]
    guided = functools.reduce(jnp.add, lax.optimization_barrier(parts))
    updated = latent[0] + step_size[:, None, None] * functools.reduce(jnp.add, parts)
    taken = lax.ppermute(updated, "section", [(0, 1)])
    taking = (section_index == 1) & (arrived_mark > 0.5)
    next_latent = jnp.where(taking[:, None, None], taken, updated)
    return (guided[None], next_latent[None])


def solution(mesh):
    placed = (
        P("section", ("groups", "blk"), "sp", None),
        P("section", ("groups", "blk"), None, "sp", None),
        P("section", ("groups", "blk"), None, "sp", None),
        P("section", ("groups", "blk"), None, "sp", None),
        P("section", None, None),
        P("section", ("groups", "blk")),
        P(("groups", "blk")),
    )
    return jax.shard_map(
        functools.partial(on_device, mesh.shape["sp"]),
        mesh=mesh,
        in_specs=placed,
        out_specs=(
            P("section", ("groups", "blk"), "sp", None),
            P("section", ("groups", "blk"), "sp", None),
        ),
        check_vma=False,
    )
```

```python
import functools

import jax
import jax.numpy as jnp
from jax import lax
from jax.experimental import pallas as pl
from jax.experimental.pallas import tpu as pltpu
from jax.sharding import PartitionSpec as P

HD = 128
CH = 64
STEPS = 40
SWITCH = 25


noise_shift = 12.0
high_guidance = 4.0
low_guidance = 3.0

VMEM = pl.BlockSpec(memory_space=pltpu.VMEM)
SMEM = pl.BlockSpec(memory_space=pltpu.SMEM)
HBM = pl.BlockSpec(memory_space=pltpu.HBM)
PAIR = 2 * HD


def noise_level(step_now):
    fraction = 1.0 - step_now.astype(jnp.float32) / STEPS
    return noise_shift * fraction / (1.0 + (noise_shift - 1.0) * fraction)


def dot_last(left, right):
    return lax.dot_general(
        left, right, (((1,), (1,)), ((), ())), preferred_element_type=jnp.float32
    )


def side_by_side(first, second):
    zero = jnp.zeros_like(first)
    return [
        jnp.concatenate([first, zero], axis=1),
        jnp.concatenate([zero, second], axis=1),
    ]


def through(moves, staged, sems_in, sems_out):
    inward = [
        pltpu.make_async_copy(source, staged.at[n], sems_in.at[n])
        for n, (source, _) in enumerate(moves)
    ]
    outward = [
        pltpu.make_async_copy(staged.at[n], target, sems_out.at[n])
        for n, (_, target) in enumerate(moves)
    ]
    for copy in inward:
        copy.start()
    for before, copy in zip(inward, outward):
        before.wait()
        copy.start()
    for copy in outward:
        copy.wait()


def pack_kernel(first, group, width, me_ref, q_ref, k_ref, *refs):
    out_refs, scratch = refs[:-3], refs[-3:]
    moves = []
    for s, out_ref in enumerate(out_refs, 1):
        start = pl.multiple_of(((me_ref[0] ^ s) & (group - 1)) * width, width)
        for n, ref in enumerate([q_ref, k_ref] if s < group else [q_ref]):
            for i in range(0, out_ref.shape[0], 2):
                moves.append(
                    (
                        ref.at[pl.ds(first + i, 2), :, pl.ds(start, width)],
                        out_ref.at[pl.ds(i, 2), :, pl.ds(n * width, width)],
                    )
                )
    through(moves, *scratch)


def project_kernel(first, group, width, me_ref, v_ref, w_ref, *out_refs):
    me = me_ref[0]
    videos = out_refs[0].shape[0]
    for s in range(group):
        lane = ((me ^ s) & (group - 1)) * width
        for p in range(width // PAIR):
            start = pl.multiple_of(lane + p * PAIR, PAIR)
            weight = w_ref[:, pl.ds(start, PAIR)]
            for v in range(videos):
                rows = []
                for way in range(2):
                    value = v_ref[2 * (first + v) + way, :, pl.ds(start, PAIR)]
                    rows += side_by_side(value[:, :HD], value[:, HD:])
                product = dot_last(weight, jnp.concatenate(rows, axis=0)).astype(jnp.bfloat16)
                half = product.shape[1] // 2
                for way in range(2):
                    out_refs[s][v, way, p // 2, :, (p % 2) * half : (p % 2 + 1) * half] = product[
                        :, way * half : (way + 1) * half
                    ]


def score_kernel(first, count, group, width, me_ref, q_ref, k_ref, *refs):
    others, outs = refs[: count - 1], refs[count - 1 :]
    whole = group == count
    lane = (me_ref[0] & (group - 1)) * width
    rows = q_ref.shape[1]
    items = outs[0].shape[0]

    def one(i, carry):
        for p in range(width // PAIR):
            own = pl.ds(pl.multiple_of(lane + p * PAIR, PAIR), PAIR)
            here = slice(p * PAIR, (p + 1) * PAIR)
            query = jnp.concatenate(
                [q_ref[2 * first + i, :, own]] + [r[i, :, here] for r in others], axis=0
            )
            keys = []
            for s in range(group):
                if s == 0:
                    key = k_ref[2 * first + i, :, own]
                else:
                    key = others[s - 1][i, :, width + p * PAIR : width + (p + 1) * PAIR]
                keys += side_by_side(key[:, :HD], key[:, HD:])
            scores = dot_last(jnp.concatenate(keys, axis=0), query) * (HD ** (-0.5))
            for h in range(2):
                places = [slice((2 * s + h) * rows, (2 * s + h + 1) * rows) for s in range(group)]
                top = functools.reduce(jnp.maximum, [scores[place] for place in places])
                top = jnp.max(top, axis=0, keepdims=True)
                exponents = [jnp.exp(scores[place] - top) for place in places]
                total = jnp.sum(
                    functools.reduce(jnp.add, exponents), axis=0, keepdims=True
                )
                if whole:
                    share = 1.0 / total
                    exponents = [(e * share).astype(jnp.bfloat16) for e in exponents]
                else:
                    outs[1][i, 2 * p + h : 2 * p + h + 1, :] = top
                    outs[2][i, 2 * p + h : 2 * p + h + 1, :] = top + jnp.log(total)
                row = (2 * (p % 2) + h) * rows
                for s, e in enumerate(exponents):
                    outs[0][i, p // 2, s, row : row + rows, :] = e
        return carry

    lax.fori_loop(0, items, one, 0)


def factors(i, top_ref, near_ref, far_ref):
    far = pltpu.roll(far_ref[i], far_ref.shape[2] // 2, 1)
    near = near_ref[i]
    most = jnp.maximum(near, far)
    return jnp.exp(top_ref[i] - most - jnp.log(jnp.exp(near - most) + jnp.exp(far - most)))


def weigh(i, group, e_ref, top_ref, near_ref, far_ref):
    factor = factors(i, top_ref, near_ref, far_ref)
    rows = e_ref.shape[3] // 4
    parts = []
    for q in range(e_ref.shape[1]):
        for s in range(group):
            for h in range(4):
                e = e_ref[i, q, s, h * rows : (h + 1) * rows, :]
                parts.append((e * factor[4 * q + h : 4 * q + h + 1]).astype(jnp.bfloat16))
    return jnp.concatenate(parts, axis=0)


def weigh_kernel(group, e_ref, top_ref, near_ref, far_ref, out_ref):
    def one(i, carry):
        out_ref[i] = weigh(i, group, e_ref, top_ref, near_ref, far_ref)
        return carry

    lax.fori_loop(0, e_ref.shape[0], one, 0)


def attend_kernel(first, count, group, parts, scale_ref, skip_ref, *refs):
    weight_refs, refs = refs[:parts], refs[parts:]
    vw_refs, refs = refs[:group], refs[group:]
    before_refs, out_refs, scratch = refs[: -count - 1], refs[-count - 1 : -1], refs[-1]
    items = weight_refs[0].shape[0]
    quads, _, columns = vw_refs[0].shape[2:]
    rows = columns // 4
    length = rows * count
    offset = first if before_refs else 0

    def one(v, carry):
        sums = []
        for way in range(2):
            i = 2 * v + way
            if parts > 1:
                weights = weigh(i, group, *weight_refs)
            else:
                weights = weight_refs[0][i]
            values = [r[v, way, q] for q in range(quads) for r in vw_refs]
            sums.append(
                jnp.dot(
                    jnp.concatenate(values, axis=1), weights, preferred_element_type=jnp.float32
                )
            )
        conditional, unconditional = sums
        guided = unconditional + scale_ref[0] * (conditional - unconditional)
        guided = jnp.where(skip_ref[first + v] == 1, conditional, guided)
        scratch[v] = jnp.concatenate([guided, guided], axis=0).T
        even = scratch[v, pl.ds(0, length // 2, stride=2), :]
        odd = scratch[v, pl.ds(1, length // 2, stride=2), :]
        column = lax.broadcasted_iota(jnp.int32, even.shape, 1)
        both = jnp.where(column < CH, even, odd)
        for s in range(count):
            out_refs[s][offset + v] = both[s * rows // 2 : (s + 1) * rows // 2]
        return carry

    for v in range(items // 2):
        one(v, 0)
    for before_ref, out_ref in zip(before_refs, out_refs):
        out_ref[0:first] = before_ref[...]


def call(kernel, outs, specs, name, scratch=(), flops=0, moved=0, space=VMEM, limit=16 << 20):
    return pl.pallas_call(
        kernel,
        out_shape=outs,
        in_specs=specs,
        out_specs=space if isinstance(space, list) else jax.tree.map(lambda _: space, outs),
        scratch_shapes=scratch,
        name=name,
        compiler_params=pltpu.CompilerParams(vmem_limit_bytes=limit),
        cost_estimate=pl.CostEstimate(flops=flops, bytes_accessed=moved, transcendentals=0),
    )


def after(array, *others):
    return lax.optimization_barrier((array, *others))[0]


def shape(*dims, dtype=jnp.bfloat16):
    return jax.ShapeDtypeStruct(dims, dtype)


def on_device(count, latent, queries, keys, values, head_weight, step_index, skip_flags):
    section_index = lax.axis_index("section")
    me = lax.axis_index("sp")[None]
    _, videos, _, rows, feature_all = queries.shape
    items = videos * 2
    length = rows * count
    query = queries[0].reshape(items, rows, feature_all)
    key = keys[0].reshape(items, rows, feature_all)
    value = values[0].reshape(items, rows, feature_all)
    late = max(1, videos // 3)
    early = videos - late

    def exchange(array, s):
        return lax.ppermute(array, "sp", [(i, i ^ s) for i in range(count)])

    def staging(number, width):
        return [
            pltpu.VMEM((number, 2, rows, width), jnp.bfloat16),
            pltpu.SemaphoreType.DMA((number,)),
            pltpu.SemaphoreType.DMA((number,)),
        ]

    def pack(me, first, many, group):
        width = feature_all // group
        wide = [(2 if s < group else 1) * width for s in range(1, count)]
        return call(
            functools.partial(pack_kernel, 2 * first, group, width),
            [shape(2 * many, rows, w) for w in wide],
            [SMEM, HBM, HBM],
            "pack",
            scratch=staging(many * (count + group - 2), width),
            moved=8 * many * rows * sum(wide),
            space=HBM,
            limit=None,
        )(me, query, key)

    def project(me, first, many, group):
        width = feature_all // group
        return call(
            functools.partial(project_kernel, first, group, width),
            [shape(many, 2, width // (2 * PAIR), CH, 4 * rows)] * group,
            [SMEM, VMEM, VMEM],
            "project",
            flops=16 * many * rows * feature_all * CH,
            moved=6 * many * rows * feature_all,
        )(me, value, head_weight[0])

    def score(me, first, many, group, arrived):
        width = feature_all // group
        heads = width // HD
        dims = (2 * many, heads // 4, group, 4 * rows, length)
        if group == count:
            outs = [shape(*dims)]
        else:
            outs = [
                shape(*dims, dtype=jnp.float32),
                shape(2 * many, heads, length, dtype=jnp.float32),
                shape(2 * many, heads, length, dtype=jnp.float32),
            ]
        return call(
            functools.partial(score_kernel, first, count, group, width),
            outs,
            [SMEM] + [VMEM] * (count + 1),
            "score",
            flops=16 * many * heads * length * length * HD,
            moved=16 * many * rows * feature_all,
        )(me, query, key, *[arrived[s] for s in range(1, count)])

    guidance = jnp.where(section_index == 0, jnp.float32(high_guidance), jnp.float32(low_guidance))
    skipping = jnp.where(section_index == 1, skip_flags, 0)

    def attend(first, many, group, weights, projected, before=()):
        total = first + many
        return call(
            functools.partial(attend_kernel, first, count, group, len(weights)),
            [shape(total, rows // 2, 2 * CH, dtype=jnp.float32)] * count,
            [SMEM, SMEM] + [VMEM] * (len(weights) + group + len(before)),
            "attend",
            scratch=[pltpu.VMEM((many, length, 2 * CH), jnp.float32)],
            flops=16 * many * feature_all * length * HD,
            moved=8 * many * rows * feature_all,
        )(guidance[None], skipping, *weights, *projected, *before)

    def weigh_all(exponents, top, near, far):
        return call(
            functools.partial(weigh_kernel, half),
            shape(exponents.shape[0], exponents.size // exponents.shape[0] // length, length),
            [VMEM] * 4,
            "weigh",
            flops=exponents.size,
            moved=6 * exponents.size,
        )(exponents, top, near, far)

    half = count // 2
    step_now = step_index[0]
    step_size = noise_level(step_now + 1) - noise_level(step_now)
    finish_mark = jnp.where(
        (section_index == 0) & (step_now + 1 == SWITCH), jnp.float32(1.0), jnp.float32(0.0)
    )
    far_shifts = list(range(count - 1, half - 1, -1))
    inner = list(range(1, half))
    first = pack(me, 0, early, half)
    second = pack(after(me, first[0]), early, late, half)
    first_values = project(after(me, second[0]), 0, early, half)
    second_values = project(after(me, second[0]), early, late, half)

    arrived = {s: exchange(first[s - 1], s) for s in range(1, count)}
    late_arrived = {s: exchange(second[s - 1], s) for s in far_shifts}
    for s in inner:
        late_arrived[s] = exchange(after(second[s - 1], arrived[half]), s)
    values_here = [first_values[0]] + [
        exchange(after(first_values[s], arrived[half]), s) for s in inner
    ]
    late_values = [second_values[0]] + [
        exchange(after(second_values[s], arrived[1]), s) for s in inner
    ]

    arrived_mark = lax.ppermute(after(finish_mark, arrived[1]), "section", [(0, 1)])
    exponents, top, near = score(after(me, arrived_mark), 0, early, half, arrived)
    weights = weigh_all(exponents, top, near, exchange(near, half))
    shares = attend(0, early, half, [weights], values_here)

    exponents, top, near = score(me, early, late, half, late_arrived)
    far = exchange(near, half)
    shares = attend(early, late, half, [exponents, top, near, far], late_values, shares)

    parts = [exchange(shares[s], s) for s in [*range(count - 1, half, -1), *range(half - 1, 0, -1), half]] + [shares[0]]
    guided = functools.reduce(jnp.add, lax.optimization_barrier(parts))
    updated = latent[0] + step_size[:, None, None] * functools.reduce(jnp.add, parts)
    taken = lax.ppermute(updated, "section", [(0, 1)])
    taking = (section_index == 1) & (arrived_mark > 0.5)
    next_latent = jnp.where(taking[:, None, None], taken, updated)
    return (guided[None], next_latent[None])


def solution(mesh):
    placed = (
        P("section", ("groups", "blk"), "sp", None),
        P("section", ("groups", "blk"), None, "sp", None),
        P("section", ("groups", "blk"), None, "sp", None),
        P("section", ("groups", "blk"), None, "sp", None),
        P("section", None, None),
        P("section", ("groups", "blk")),
        P(("groups", "blk")),
    )
    return jax.shard_map(
        functools.partial(on_device, mesh.shape["sp"]),
        mesh=mesh,
        in_specs=placed,
        out_specs=(
            P("section", ("groups", "blk"), "sp", None),
            P("section", ("groups", "blk"), "sp", None),
        ),
        check_vma=False,
    )
```
